256 devices in a mesh: slab: 16 (over y, x), tile: 4 (over z_lo, core), view: 4 (over z_hi).
Axes of the slice: x: 4, y: 4, z: 8 (z_hi: 4, z_lo: 2; z = z_hi * 2 + z_lo), core: 2. Of those that a mesh axis runs over, the one named last changes fastest.
Arguments:
- estimate: float32 [256, 256, 128], P('slab', 'tile'), may hold values from 0.25 to 4
- measured: float32 [4, 256, 256, 128], P('view', 'slab', 'tile'), may hold values from 0.25 to 4
- psf_taps: float32 [4, 3, 31], P('view'), may hold values from 0.3 to 1
- plane_source: int32 [4, 256], P('view'), may hold values from 0 to 255, as said below
- plane_shift: int32 [4, 256], P('view'), may hold values from 0 to 127
Outputs:
- new_estimate: float32 [256, 256, 128], P('slab', 'tile', 'view')
The draws below stay inside these ranges and needn't reach their ends.
Inputs may be any that keep to these rules, and one draw needn't show every extreme that they name: `plane_source`: for each view, the 16 camera planes of one aligned block of 16 take their sample planes from 8 different aligned blocks of 16 sample planes, exactly 2 from each; a sample plane may be shown several times or not at all.
All inputs are finite; a program needn't handle non-finite values.
Results may differ from the reference program's by a relative error of at most 0.0001.
Values sent between devices are 32-bit elements; how exact they have to be, the bound alone decides.
A program may use at most 64 MiB of HBM per device.

```python
import math
import jax
import jax.numpy as jnp
from jax import lax

ZD = 16
X = 128
TAPS = 31
VIEWS = 4
Z = 256
Y = 256
CAP = 2


def draw_plane_source(key, part):
    stride_key, within_key = jax.random.split(jax.random.fold_in(key, 7))
    devices = Z // ZD
    strides = jax.random.randint(stride_key, (VIEWS, 1, 1), 1, max(devices, 2))
    camera = jnp.broadcast_to(jnp.arange(devices, dtype=jnp.int32)[None, :, None], (VIEWS, devices, ZD))
    slot_index = jnp.broadcast_to(jnp.arange(ZD, dtype=jnp.int32)[None, None, :], (VIEWS, devices, ZD))
    owners = jnp.mod(camera * strides + slot_index // CAP, devices)
    within = jax.random.randint(within_key, (VIEWS, devices, ZD), 0, ZD)
    return (owners * ZD + within).reshape(VIEWS, Z).astype(jnp.int32)


def touch_ends(result, own_key, least, high):
    spot = [jax.random.randint(jax.random.fold_in(own_key, axis), (), 0, length) for axis, length in enumerate(result.shape)]
    widest = result.shape.index(max(result.shape))
    next_to = spot[:widest] + [(spot[widest] + 1) % result.shape[widest]] + spot[widest + 1:]
    return result.at[tuple(spot)].set(least).at[tuple(next_to)].set(high)


def shard_levels(key, extent, cuts, least, high):
    factor_of, own = 1.0, jax.random.fold_in(key, 6)
    for position, parts in cuts:
        draws = jnp.exp(jax.random.uniform(jax.random.fold_in(own, position), (parts,), jnp.float32, least / len(cuts), high / len(cuts)))
        factor_of = factor_of * jnp.repeat(draws, extent[position] // parts).reshape([-1 if axis == position else 1 for axis in range(len(extent))])
    return factor_of


def setup_inputs(seed: int = 0) -> dict:
    key_list = jax.random.split(jax.random.key(seed), 6)
    return {
        "estimate": jnp.clip(jnp.exp(math.log(4.0) - 2.7725887 * jax.random.uniform(key_list[0], (Z, Y, X), jnp.float32) ** shard_levels(key_list[0], (Z, Y, X), ((0, 16), (1, 4)), -0.2, 0.2)), 0.25, 4.0),
        "measured": jnp.clip(jnp.exp(math.log(4.0) - 2.7725887 * jax.random.uniform(key_list[1], (VIEWS, Z, Y, X), jnp.float32) ** shard_levels(key_list[1], (VIEWS, Z, Y, X), ((0, 4), (1, 16), (2, 4)), -0.2, 0.2)), 0.25, 4.0),
        "psf_taps": jnp.clip(jnp.exp(math.log(1.0) - 1.2039728 * jax.random.uniform(key_list[2], (VIEWS, 3, TAPS), jnp.float32) ** shard_levels(key_list[2], (VIEWS, 3, TAPS), ((0, 4),), -0.2, 0.2)), 0.3, 1.0),
        "plane_source": draw_plane_source(jax.random.fold_in(key_list[5], 71), 0),
        "plane_shift": touch_ends(jax.random.randint(key_list[4], (VIEWS, Z), 0, X), jax.random.fold_in(key_list[4], 1), 0, X - 1).astype(jnp.int32),
    }


def cyclic_blur(volume, kernel, axis, direction):
    radius = (kernel.shape[0] - 1) // 2
    summed = jnp.zeros_like(volume)
    for tap_index in range(kernel.shape[0]):
        summed = summed + kernel[tap_index] * jnp.roll(volume, direction * (radius - tap_index), axis=axis)
    return summed


def reference(estimate, measured, psf_taps, plane_source, plane_shift):
    kernels = psf_taps / jnp.sum(psf_taps, axis=2, keepdims=True)
    x_width = estimate.shape[2]
    col_index = lax.broadcasted_iota(jnp.int32, (1, 1, x_width), 2)
    summed = jnp.zeros_like(estimate)
    for view_index in range(VIEWS):
        blurred = cyclic_blur(estimate, kernels[view_index, 0], 0, 1)
        blurred = cyclic_blur(blurred, kernels[view_index, 1], 1, 1)
        blurred = cyclic_blur(blurred, kernels[view_index, 2], 2, 1)
        sources = plane_source[view_index].astype(jnp.int32)
        shifts = plane_shift[view_index].astype(jnp.int32)
        camera = jnp.take(blurred, sources, axis=0)
        x_index = jnp.mod(col_index - shifts[:, None, None], x_width).astype(jnp.int32)
        forward = jnp.take_along_axis(camera, jnp.broadcast_to(x_index, camera.shape), axis=2)
        ratio_planes = measured[view_index] / forward
        back_index = jnp.mod(col_index + shifts[:, None, None], x_width).astype(jnp.int32)
        unsheared = jnp.take_along_axis(ratio_planes, jnp.broadcast_to(back_index, camera.shape), axis=2)
        pulled = jax.ops.segment_sum(unsheared, sources, num_segments=estimate.shape[0])
        correction = cyclic_blur(pulled, kernels[view_index, 2], 2, -1)
        correction = cyclic_blur(correction, kernels[view_index, 1], 1, -1)
        correction = cyclic_blur(correction, kernels[view_index, 0], 0, -1)
        summed = summed + correction
    return estimate * summed / VIEWS
```

```python
import functools

import jax
import jax.numpy as jnp
from jax import lax
from jax.experimental import pallas as pl
from jax.experimental.pallas import tpu as pltpu
from jax.sharding import PartitionSpec as P

MESH = pl.DeviceIdType.MESH
EXACT = lax.Precision.HIGHEST
TAPS = 31
RADIUS = 15
HALO = 16


def dot(a, b):
    return jnp.dot(a, b, precision=EXACT, preferred_element_type=jnp.float32)


def circulant(taps, flip):
    total = taps[0]
    for t in range(1, TAPS):
        total = total + taps[t]
    row = lax.broadcasted_iota(jnp.int32, (128, 128), 0)
    col = lax.broadcasted_iota(jnp.int32, (128, 128), 1)
    off = lax.rem(col - row + RADIUS + 128, 128)
    out = jnp.zeros((128, 128), jnp.float32)
    for t in range(TAPS):
        out = jnp.where(off == t, taps[TAPS - 1 - t if flip else t], out)
    return out / jnp.full((128, 128), total)


def wide(block):
    row = lax.broadcasted_iota(jnp.int32, (128, 128), 0)
    col = lax.broadcasted_iota(jnp.int32, (128, 128), 1)
    near = jnp.abs(row - col) <= RADIUS
    a = jnp.where(near, block, 0.0)
    b = jnp.where(near, 0.0, block)
    return jnp.concatenate(
        [jnp.concatenate([a, b], axis=1), jnp.concatenate([b, a], axis=1)], axis=0
    )


def kernel(
    taps_ref, shift_ref, source_ref, est_ref, meas_ref, out_ref,
    ext, meas, packed_m, packed_e, got_m, got_e, forth, seen, rolled, table, tables,
    edges, arrived, acc, spread, quarter, band_y, mix_x, band_z, back_z, pick, mix_back,
    local_sem, halo_send, halo_recv, tap_send, tap_recv, m_send, m_recv, e_send, e_recv,
    p_send, p_recv, edge_send, edge_recv, ready,
):
    slab, tile, view = lax.axis_index("slab"), lax.axis_index("tile"), lax.axis_index("view")
    side = 4
    sy, sx = slab // side, lax.rem(slab, side)
    up, down = lax.rem(tile + 1, 4), lax.rem(tile + 3, 4)

    def slab_at(d):
        dy, dx = d // side, lax.rem(d, side)
        return lax.rem(sy + dy, side) * side + lax.rem(sx + dx, side)

    def view_at(d):
        return lax.rem(view + d, 4)

    own_est = pltpu.make_async_copy(est_ref, ext.at[:, pl.ds(HALO, 64), :], local_sem.at[0])
    own_meas = pltpu.make_async_copy(meas_ref.at[0], meas, local_sem.at[1])
    own_est.start()
    own_meas.start()

    barrier = pltpu.get_barrier_semaphore()

    def greet(d, _):
        pl.semaphore_signal(
            barrier, inc=1, device_id=(slab_at(d), tile, view), device_id_type=MESH
        )
        return 0

    lax.fori_loop(1, 16, greet, 0)
    for t in (up, down):
        pl.semaphore_signal(barrier, inc=1, device_id=(slab, t, view), device_id_type=MESH)
    for d in (1, 2, 3):
        pl.semaphore_signal(
            barrier, inc=1, device_id=(slab, tile, view_at(d)), device_id_type=MESH
        )

    taps_y = [taps_ref[0, 1, t] for t in range(TAPS)]
    total_y = taps_y[0]
    for t in range(1, TAPS):
        total_y = total_y + taps_y[t]
    for t in range(TAPS):
        table[pl.ds(t, 1), :] = jnp.full((1, 128), taps_y[t])
    table[pl.ds(TAPS, 1), :] = jnp.zeros((1, 128), jnp.float32)
    table[...] = table[...] / jnp.full((32, 128), total_y)

    pl.semaphore_wait(barrier, 20)

    to_up = pltpu.make_async_remote_copy(
        src_ref=est_ref.at[:, pl.ds(64 - HALO, HALO), :], dst_ref=ext.at[:, pl.ds(0, HALO), :],
        send_sem=halo_send.at[0], recv_sem=halo_recv.at[0],
        device_id=(slab, up, view), device_id_type=MESH,
    )
    to_down = pltpu.make_async_remote_copy(
        src_ref=est_ref.at[:, pl.ds(0, HALO), :], dst_ref=ext.at[:, pl.ds(64 + HALO, HALO), :],
        send_sem=halo_send.at[1], recv_sem=halo_recv.at[1],
        device_id=(slab, down, view), device_id_type=MESH,
    )
    to_up.start()
    to_down.start()
    tap_copies = []
    for d in (1, 2, 3):
        c = pltpu.make_async_remote_copy(
            src_ref=table, dst_ref=tables.at[view],
            send_sem=tap_send.at[d], recv_sem=tap_recv.at[d],
            device_id=(slab, tile, view_at(d)), device_id_type=MESH,
        )
        c.start()
        tap_copies.append(c)
        pl.semaphore_signal(
            ready, inc=1, device_id=(slab, tile, view_at(d)), device_id_type=MESH
        )
    tables[view] = table[...]

    own_meas.wait()
    for j in range(16):
        amount = lax.rem(128 - shift_ref[0, slab * 16 + j], 128)
        plane = pltpu.roll(meas[j], amount, 1)
        packed_m[pl.ds(j, 64, stride=16), :] = plane

    def m_copy(d):
        to = slab_at(d)
        return pltpu.make_async_remote_copy(
            src_ref=packed_m3.at[pl.ds(to * 4, 4)],
            dst_ref=got_m.at[:, pl.ds(pl.multiple_of(slab * 16, 16), 16), :],
            send_sem=m_send.at[d], recv_sem=m_recv.at[d],
            device_id=(to, tile, view), device_id_type=MESH,
        )

    def e_copy(d):
        to = slab_at(d)
        return pltpu.make_async_remote_copy(
            src_ref=packed_e3.at[pl.ds(to * 4, 4)],
            dst_ref=got_e.at[:, pl.ds(pl.multiple_of(slab * 16, 16), 16), :],
            send_sem=e_send.at[d], recv_sem=e_recv.at[d],
            device_id=(to, tile, view), device_id_type=MESH,
        )

    packed_m3 = packed_m.reshape(64, 16, 128)
    packed_e3 = packed_e.reshape(64, 16, 128)

    def start_m(d, _):
        m_copy(d).start()
        return 0

    lax.fori_loop(1, 16, start_m, 0)
    mine = pl.ds(pl.multiple_of(slab * 16, 16), 16)
    for k in range(4):
        got_m[k, mine, :] = packed_m3[slab * 4 + k]

    band_y[...] = circulant([taps_ref[0, 1, t] for t in range(TAPS)], False)
    mix_x[...] = circulant([taps_ref[0, 2, t] for t in range(TAPS)], True)

    own_est.wait()
    to_up.wait()
    to_down.wait()
    flat = jnp.concatenate([ext[z] for z in range(16)], axis=1)
    by_y = dot(band_y[HALO : 64 + HALO, 0:96], flat)
    tall = jnp.concatenate([by_y[:, 128 * z : 128 * z + 128] for z in range(16)], axis=0)
    by_x = dot(tall, mix_x[...])
    for z in range(16):
        packed_e[pl.ds(z, 64, stride=16), :] = by_x[64 * z : 64 * z + 64, :]

    def start_e(d, _):
        e_copy(d).start()
        return 0

    lax.fori_loop(1, 16, start_e, 0)
    for k in range(4):
        got_e[k, mine, :] = packed_e3[slab * 4 + k]

    taps_z = [taps_ref[0, 0, t] for t in range(TAPS)]
    band_z[...] = wide(circulant(taps_z, False))
    back_z[...] = wide(circulant(taps_z, True))
    plane_of = lax.broadcasted_iota(jnp.int32, (256, 256), 0)
    pick[...] = (jnp.broadcast_to(source_ref[...], (256, 256)) == plane_of).astype(jnp.float32)
    x_adjoint = circulant([taps_ref[0, 2, t] for t in range(TAPS)], False)
    lane = lax.broadcasted_iota(jnp.int32, (128, 128), 1)
    for k in range(4):
        for w in range(4):
            turned = x_adjoint if k == w else pltpu.roll(x_adjoint, (32 * (k - w)) % 128, 1)
            mix_back[128 * k : 128 * k + 128, 128 * w : 128 * w + 128] = jnp.where(
                (lane >= 32 * k) & (lane < 32 * k + 32), turned, 0.0
            )
    for z in range(16):
        quarter[z] = pltpu.roll(ext[z, HALO : 64 + HALO, :], lax.rem(128 - 32 * view, 128), 1)
    for v in range(4):
        for r in range(4):
            rolled[v, r, 0:8] = jnp.zeros((8, 16, 128), jnp.float32)
            rolled[v, r, 23:31] = jnp.zeros((8, 16, 128), jnp.float32)

    def wait_m(d, _):
        m_copy(d).wait()
        return 0

    lax.fori_loop(1, 16, wait_m, 0)
    routed = dot(pick[...], jnp.concatenate([got_m[k] for k in range(4)], axis=1))

    def wait_e(d, _):
        e_copy(d).wait()
        return 0

    lax.fori_loop(1, 16, wait_e, 0)
    blurred = dot(band_z[...], jnp.concatenate([got_e[k] for k in range(4)], axis=1))
    pulled = dot(back_z[...], routed / blurred)
    by_quarter = dot(pulled, mix_back[...])
    for w in range(4):
        forth[w] = by_quarter[:, 128 * w : 128 * w + 128]

    pl.semaphore_wait(ready, 3)

    def p_copy(ds, dv):
        to, w = slab_at(ds), view_at(dv)
        return pltpu.make_async_remote_copy(
            src_ref=forth.at[w, pl.ds(pl.multiple_of(to * 16, 16), 16), :],
            dst_ref=seen.at[view, slab],
            send_sem=p_send.at[dv, ds], recv_sem=p_recv.at[dv, ds],
            device_id=(to, tile, w), device_id_type=MESH,
        )

    def start_p(ds, _):
        for dv in (2, 1, 3):
            p_copy(ds, dv).start()

        @pl.when(ds > 0)
        def _():
            p_copy(ds, 0).start()

        return 0

    lax.fori_loop(0, 16, start_p, 0)
    seen[view, slab] = forth[view, mine, :]
    for c in tap_copies:
        c.wait()

    def wait_p(ds, _):
        for dv in (2, 1, 3):
            p_copy(ds, dv).wait()

        @pl.when(ds > 0)
        def _():
            p_copy(ds, 0).wait()

        return 0

    lax.fori_loop(0, 16, wait_p, 0)

    lanes = lax.broadcasted_iota(jnp.int32, (16, 16, 128), 2)
    for v in range(4):
        block = seen[v]
        rolled[v, 0, 8:24] = block
        for r in (1, 2, 3):
            turned = pltpu.roll(block.reshape(256, 128), 128 - 32 * r, 1).reshape(16, 16, 128)
            keep = lanes < 128 - 32 * r
            rolled[v, r, 8:24] = jnp.where(keep, turned, 0.0)
            follow = jnp.where(keep, 0.0, turned)
            rolled[v, r, 7:23] = rolled[v, r, 7:23] + follow

    def gather_rows(base, lo, hi):
        total = [jnp.zeros((16, 128), jnp.float32) for _ in range(4)]
        for v in range(4):
            for d in range(lo, hi + 1):
                m, r = d // 4, d % 4
                c = jnp.broadcast_to(tables[v, pl.ds(RADIUS - d, 1), :], (16, 128))
                for j in range(4):
                    total[j] = total[j] + c * rolled[v, r, base + j + m + 8]
        return total

    low = gather_rows(-4, 0, RADIUS)
    high = gather_rows(16, -RADIUS, -1)
    for j in range(4):
        edges[0, j] = low[j]
        edges[1, j] = high[j]
    edge_down = pltpu.make_async_remote_copy(
        src_ref=edges.at[0], dst_ref=arrived.at[0],
        send_sem=edge_send.at[0], recv_sem=edge_recv.at[0],
        device_id=(slab, down, view), device_id_type=MESH,
    )
    edge_up = pltpu.make_async_remote_copy(
        src_ref=edges.at[1], dst_ref=arrived.at[1],
        send_sem=edge_send.at[1], recv_sem=edge_recv.at[1],
        device_id=(slab, up, view), device_id_type=MESH,
    )
    edge_down.start()
    edge_up.start()

    def chunk(c, _):
        rows = gather_rows(c * 4, -RADIUS, RADIUS)
        for j in range(4):
            acc[c * 4 + j] = rows[j]
        return 0

    lax.fori_loop(0, 4, chunk, 0)
    edge_down.wait()
    edge_up.wait()
    acc[12:16] = acc[12:16] + arrived[0]
    acc[0:4] = acc[0:4] + arrived[1]

    for s in range(16):
        rows = acc[s]
        for k in range(4):
            part = rows if k == 0 else pltpu.roll(rows, 128 - 32 * k, 1)
            spread[pl.ds(4 * s + k, 16, stride=64), :] = part
    for z in range(16):
        summed = spread[64 * z : 64 * z + 64, :]
        out_ref[z] = (quarter[z] * summed * 0.25)[:, 0:32]


def local(estimate, measured, psf_taps, plane_source, plane_shift):
    f32 = jnp.float32
    dma = pltpu.SemaphoreType.DMA
    smem = pl.BlockSpec(memory_space=pltpu.SMEM)
    vmem = pl.BlockSpec(memory_space=pltpu.VMEM)
    hbm = pl.BlockSpec(memory_space=pl.ANY)
    return pl.pallas_call(
        kernel,
        name="update",
        out_shape=jax.ShapeDtypeStruct((16, 64, 32), f32),
        in_specs=[smem, smem, vmem, hbm, hbm],
        out_specs=vmem,
        scratch_shapes=[
            pltpu.VMEM((16, 96, 128), f32),
            pltpu.VMEM((16, 64, 128), f32),
            pltpu.VMEM((1024, 128), f32),
            pltpu.VMEM((1024, 128), f32),
            pltpu.VMEM((4, 256, 128), f32),
            pltpu.VMEM((4, 256, 128), f32),
            pltpu.VMEM((4, 256, 128), f32),
            pltpu.VMEM((4, 16, 16, 128), f32),
            pltpu.VMEM((4, 4, 31, 16, 128), f32),
            pltpu.VMEM((32, 128), f32),
            pltpu.VMEM((4, 32, 128), f32),
            pltpu.VMEM((2, 4, 16, 128), f32),
            pltpu.VMEM((2, 4, 16, 128), f32),
            pltpu.VMEM((16, 16, 128), f32),
            pltpu.VMEM((1024, 128), f32),
            pltpu.VMEM((16, 64, 128), f32),
            pltpu.VMEM((128, 128), f32),
            pltpu.VMEM((128, 128), f32),
            pltpu.VMEM((256, 256), f32),
            pltpu.VMEM((256, 256), f32),
            pltpu.VMEM((256, 256), f32),
            pltpu.VMEM((512, 512), f32),
            dma((2,)), dma((2,)), dma((2,)), dma((4,)), dma((4,)),
            dma((16,)), dma((16,)), dma((16,)), dma((16,)),
            dma((4, 16)), dma((4, 16)), dma((2,)), dma((2,)),
            pltpu.SemaphoreType.REGULAR,
        ],
        compiler_params=pltpu.CompilerParams(
            collective_id=0, has_side_effects=True, vmem_limit_bytes=56 * 2**20
        ),
    )(psf_taps, plane_shift, plane_source, estimate, measured)


def solution(mesh):
    in_specs = (
        P("slab", "tile", None),
        P("view", "slab", "tile", None),
        P("view", None, None),
        P("view", None),
        P("view", None),
    )
    return jax.shard_map(
        local, mesh=mesh, in_specs=in_specs, out_specs=P("slab", "tile", "view"), check_vma=False
    )
```

```python
import jax
import jax.numpy as jnp
from jax import lax
from jax.experimental import pallas as pl
from jax.experimental.pallas import tpu as pltpu
from jax.sharding import PartitionSpec as P

MESH = pl.DeviceIdType.MESH
F32 = jnp.float32
B16 = jnp.bfloat16
TAPS = 31
RADIUS = 15
HALO = 16


def split(x):
    high = x.astype(B16)
    return high, (x - high.astype(F32)).astype(B16)


def left3(x):
    high, low = split(x)
    return jnp.concatenate([high, high, low], axis=1)


def right3(x):
    high, low = split(x)
    return jnp.concatenate([high, low, high], axis=0)


def dot(a, b):
    return jnp.dot(a, b, preferred_element_type=F32)


def circulant(taps, flip):
    total = taps[0]
    for t in range(1, TAPS):
        total = total + taps[t]
    row = lax.broadcasted_iota(jnp.int32, (128, 128), 0)
    col = lax.broadcasted_iota(jnp.int32, (128, 128), 1)
    off = lax.rem(col - row + RADIUS + 128, 128)
    out = jnp.zeros((128, 128), F32)
    for t in range(TAPS):
        out = jnp.where(off == t, taps[TAPS - 1 - t if flip else t], out)
    return out / jnp.full((128, 128), total)


def wide(block):
    row = lax.broadcasted_iota(jnp.int32, (128, 128), 0)
    col = lax.broadcasted_iota(jnp.int32, (128, 128), 1)
    near = jnp.abs(row - col) <= RADIUS
    a = jnp.where(near, block, 0.0)
    b = jnp.where(near, 0.0, block)
    return jnp.concatenate(
        [jnp.concatenate([a, b], axis=1), jnp.concatenate([b, a], axis=1)], axis=0
    )


def kernel(
    taps_ref, shift_ref, source_ref, est_ref, meas_ref, out_ref,
    ext, meas, pack_m, pack_e, got_m, got_e, forth, seen, table, tables, coefs,
    sums, edges, arrived, final, quarter, band_y, mix_x, band_z, back_z, pick, mix_back,
    local_sem, halo_send, halo_recv, tap_send, tap_recv, m_send, m_recv, e_send, e_recv,
    p_send, p_recv, edge_send, edge_recv, ready,
):
    slab, tile, view = lax.axis_index("slab"), lax.axis_index("tile"), lax.axis_index("view")
    side = 4
    sy, sx = slab // side, lax.rem(slab, side)
    up, down = lax.rem(tile + 1, 4), lax.rem(tile + 3, 4)

    def slab_at(d):
        dy, dx = d // side, lax.rem(d, side)
        return lax.rem(sy + dy, side) * side + lax.rem(sx + dx, side)

    def view_at(d):
        return lax.rem(view + d, 4)

    own_est = pltpu.make_async_copy(est_ref, ext.at[:, pl.ds(HALO, 64), :], local_sem.at[0])
    own_meas = pltpu.make_async_copy(meas_ref.at[0], meas, local_sem.at[1])
    own_est.start()
    own_meas.start()

    barrier = pltpu.get_barrier_semaphore()
    for d in (2, 1, 3):
        pl.semaphore_signal(
            barrier, inc=1, device_id=(slab, tile, view_at(d)), device_id_type=MESH
        )

    def greet(d, _):
        pl.semaphore_signal(
            barrier, inc=1, device_id=(slab_at(d), tile, view), device_id_type=MESH
        )
        return 0

    lax.fori_loop(1, 16, greet, 0)
    for t in (up, down):
        pl.semaphore_signal(barrier, inc=1, device_id=(slab, t, view), device_id_type=MESH)

    taps_z = [taps_ref[0, 0, t] for t in range(TAPS)]
    taps_y = [taps_ref[1, 0, t] for t in range(TAPS)]
    taps_x = [taps_ref[2, 0, t] for t in range(TAPS)]
    total_y = taps_y[0]
    for t in range(1, TAPS):
        total_y = total_y + taps_y[t]
    for t in range(TAPS):
        table[pl.ds(t, 1), :] = jnp.full((1, 128), taps_y[t])
    table[pl.ds(TAPS, 1), :] = jnp.zeros((1, 128), F32)
    table[...] = table[...] / jnp.full((32, 128), total_y)
    tables[view] = table[...]

    band_y[...] = circulant(taps_y, False)
    mix_x[...] = right3(circulant(taps_x, True))

    own_meas.wait()
    for j in range(16):
        amount = lax.rem(128 - shift_ref[0, slab * 16 + j], 128)
        plane = pltpu.roll(meas[j], amount, 1)
        pack_m[0, pl.ds(j, 32, stride=16), :] = plane[16:48]
        pack_m[1, pl.ds(j, 16, stride=16), :] = plane[0:16]
        pack_m[1, pl.ds(256 + j, 16, stride=16), :] = plane[48:64]

    def blur_rows(chunk, band, flat):
        by_y = dot(left3(band), right3(flat))
        tall = jnp.concatenate([by_y[:, 128 * z : 128 * z + 128] for z in range(16)], axis=0)
        by_x = dot(left3(tall), mix_x[...])
        for z in range(16):
            pack_e[chunk, pl.ds(z, 32, stride=16), :] = by_x[32 * z : 32 * z + 32, :]

    own_est.wait()
    blur_rows(
        0,
        band_y[32:64, 16:80],
        jnp.concatenate([ext[z, HALO : 64 + HALO, :] for z in range(16)], axis=1),
    )

    pl.semaphore_wait(barrier, 20)

    to_up = pltpu.make_async_remote_copy(
        src_ref=est_ref.at[:, pl.ds(64 - HALO, HALO), :], dst_ref=ext.at[:, pl.ds(0, HALO), :],
        send_sem=halo_send.at[0], recv_sem=halo_recv.at[0],
        device_id=(slab, up, view), device_id_type=MESH,
    )
    to_down = pltpu.make_async_remote_copy(
        src_ref=est_ref.at[:, pl.ds(0, HALO), :], dst_ref=ext.at[:, pl.ds(64 + HALO, HALO), :],
        send_sem=halo_send.at[1], recv_sem=halo_recv.at[1],
        device_id=(slab, down, view), device_id_type=MESH,
    )
    to_up.start()
    to_down.start()

    mine = pl.ds(pl.multiple_of(slab * 16, 16), 16)
    pack_m5 = pack_m.reshape(2, 2, 16, 16, 128)
    pack_e5 = pack_e.reshape(2, 2, 16, 16, 128)

    def m_copy(chunk, d):
        to = slab_at(d)
        return pltpu.make_async_remote_copy(
            src_ref=pack_m5.at[chunk, :, to], dst_ref=got_m.at[chunk, :, mine, :],
            send_sem=m_send.at[chunk, d], recv_sem=m_recv.at[chunk, d],
            device_id=(to, tile, view), device_id_type=MESH,
        )

    def e_copy(chunk, d):
        to = slab_at(d)
        return pltpu.make_async_remote_copy(
            src_ref=pack_e5.at[chunk, :, to], dst_ref=got_e.at[chunk, :, mine, :],
            send_sem=e_send.at[chunk, d], recv_sem=e_recv.at[chunk, d],
            device_id=(to, tile, view), device_id_type=MESH,
        )

    def exchange(copy, pack, got, chunk):
        def start(d, _):
            copy(chunk, d).start()
            return 0

        lax.fori_loop(1, 16, start, 0)
        for k in range(2):
            got[chunk, k, mine, :] = pack[chunk, k, slab]

    def await_all(copy, chunk):
        def wait(d, _):
            copy(chunk, d).wait()
            return 0

        lax.fori_loop(1, 16, wait, 0)

    exchange(m_copy, pack_m5, got_m, 0)
    exchange(e_copy, pack_e5, got_e, 0)
    tap_copies = []
    for d in (2, 1, 3):
        c = pltpu.make_async_remote_copy(
            src_ref=table, dst_ref=tables.at[view],
            send_sem=tap_send.at[d], recv_sem=tap_recv.at[d],
            device_id=(slab, tile, view_at(d)), device_id_type=MESH,
        )
        c.start()
        tap_copies.append(c)
        pl.semaphore_signal(
            ready, inc=1, device_id=(slab, tile, view_at(d)), device_id_type=MESH
        )
    exchange(m_copy, pack_m5, got_m, 1)

    band_z[...] = left3(wide(circulant(taps_z, False)))
    back_z[...] = left3(wide(circulant(taps_z, True)))
    plane_of = lax.broadcasted_iota(jnp.int32, (256, 256), 0)
    shown = jnp.where(jnp.broadcast_to(source_ref[...], (256, 256)) == plane_of, 1.0, 0.0)
    shown = shown.astype(B16)
    pick[...] = jnp.concatenate([shown, shown], axis=1)
    x_high, x_low = split(circulant(taps_x, False))
    x_high, x_low = x_high.astype(F32), x_low.astype(F32)
    lane = lax.broadcasted_iota(jnp.int32, (128, 128), 1)
    for b in range(4):
        inside = (lane >= 32 * b) & (lane < 32 * b + 32)
        for w in range(4):
            for part, rows in ((x_high, (0, 1024)), (x_low, (512,))):
                turned = part if b == w else pltpu.roll(part, (32 * (b - w)) % 128, 1)
                block = jnp.where(inside, turned, 0.0).astype(B16)
                for row in rows:
                    at = row + 128 * b
                    mix_back[at : at + 128, 128 * w : 128 * w + 128] = block

    to_up.wait()
    to_down.wait()
    blur_rows(
        1,
        jnp.concatenate([band_y[16:32, 0:96], band_y[64:80, 0:96]], axis=0),
        jnp.concatenate([ext[z] for z in range(16)], axis=1),
    )
    exchange(e_copy, pack_e5, got_e, 1)

    def p_copy(chunk, ds, dv):
        to, w = slab_at(ds), view_at(dv)
        return pltpu.make_async_remote_copy(
            src_ref=forth.at[chunk, w, to], dst_ref=seen.at[chunk, view, slab],
            send_sem=p_send.at[chunk, dv, ds], recv_sem=p_recv.at[chunk, dv, ds],
            device_id=(to, tile, w), device_id_type=MESH,
        )

    def process(chunk):
        await_all(m_copy, chunk)
        m = jnp.concatenate([got_m[chunk, 0], got_m[chunk, 1]], axis=1)
        m_high, m_low = split(m)
        routed = dot(pick[...], jnp.concatenate([m_high, m_low], axis=0))
        await_all(e_copy, chunk)
        e = jnp.concatenate([got_e[chunk, 0], got_e[chunk, 1]], axis=1)
        blurred = dot(band_z[...], right3(e))
        pulled = dot(back_z[...], right3(routed / blurred)).reshape(16, 2, 8, 256)
        halves = jnp.concatenate(
            [pulled[:, 0].reshape(128, 256), pulled[:, 1].reshape(128, 256)], axis=1
        )
        by_quarter = dot(left3(halves), mix_back[...])
        for w in range(4):
            forth[chunk, w] = by_quarter[:, 128 * w : 128 * w + 128].reshape(16, 8, 128)
        if chunk == 0:
            pl.semaphore_wait(ready, 3)

        def start(i, _):
            ds = lax.rem(i, 16)
            for dv in (2, 1, 3):
                p_copy(chunk, ds, dv).start()
            return 0

        def start_own(ds, _):
            p_copy(chunk, ds, 0).start()
            return 0

        lax.fori_loop(1, 17, start, 0)
        lax.fori_loop(1, 16, start_own, 0)
        seen[chunk, view, slab] = forth[chunk, view, slab]

    process(0)
    process(1)

    for z in range(16):
        quarter[z] = jnp.transpose(ext[z, HALO : 64 + HALO, :])
    for c in tap_copies:
        c.wait()
    for v in range(4):
        for t in range(TAPS):
            coefs[v, t] = jnp.broadcast_to(tables[v, pl.ds(t, 1), :], (8, 128))

    def await_view(chunk, dv):
        def wait(ds, _):
            p_copy(chunk, ds, dv).wait()
            return 0

        lax.fori_loop(1, 16, wait, 0)
        if dv:
            p_copy(chunk, 0, dv).wait()

    def accumulate(chunk, dv, kind):
        v = lax.rem(view + 4 - dv, 4)
        shift = (0, 16, -16)[kind]
        for s in range(16):
            total = sums[chunk, kind, s] if dv else None
            for source in range(16):
                d = source + shift - s
                if abs(d) <= RADIUS:
                    term = coefs[v, RADIUS - d] * seen[chunk, v, source]
                    total = term if total is None else total + term
            if total is not None:
                sums[chunk, kind, s] = total

    sums[0, 1, 0] = jnp.zeros((8, 128), F32)
    sums[1, 1, 0] = jnp.zeros((8, 128), F32)
    sums[0, 2, 15] = jnp.zeros((8, 128), F32)
    sums[1, 2, 15] = jnp.zeros((8, 128), F32)
    for chunk in range(2):
        for dv in (0, 2, 1, 3):
            await_view(chunk, dv)
            accumulate(chunk, dv, 1)
            accumulate(chunk, dv, 2)
            if (chunk, dv) != (1, 3):
                accumulate(chunk, dv, 0)

    even = lax.rem(lax.broadcasted_iota(jnp.int32, (8, 128), 1) // 32, 2) == 0
    for s in range(8):
        edges[0, s] = jnp.where(even, sums[1, 1, s + 8], pltpu.roll(sums[1, 1, s], 32, 1))
        edges[1, s] = jnp.where(even, pltpu.roll(sums[1, 2, s], 96, 1), sums[1, 2, s + 8])
    edge_down = pltpu.make_async_remote_copy(
        src_ref=edges.at[0], dst_ref=arrived.at[0],
        send_sem=edge_send.at[0], recv_sem=edge_recv.at[0],
        device_id=(slab, down, view), device_id_type=MESH,
    )
    edge_up = pltpu.make_async_remote_copy(
        src_ref=edges.at[1], dst_ref=arrived.at[1],
        send_sem=edge_send.at[1], recv_sem=edge_recv.at[1],
        device_id=(slab, up, view), device_id_type=MESH,
    )
    edge_down.start()
    edge_up.start()
    accumulate(1, 3, 0)
    for s in range(16):
        above_0, above_1 = sums[0, 1, s], sums[1, 1, s]
        below_0, below_1 = sums[0, 2, s], sums[1, 2, s]
        final[0, s] = sums[0, 0, s] + jnp.where(
            even,
            pltpu.roll(above_0, 96, 1) + below_1,
            above_1 + pltpu.roll(below_0, 32, 1),
        )
        final[1, s] = sums[1, 0, s] + jnp.where(even, above_0, below_0)
    edge_down.wait()
    edge_up.wait()
    for s in range(8):
        from_up, from_down = arrived[0, s], arrived[1, s]
        final[1, s] = final[1, s] + jnp.where(even, from_down, from_up)
        final[1, s + 8] = final[1, s + 8] + jnp.where(
            even, pltpu.roll(from_down, 96, 1), pltpu.roll(from_up, 32, 1)
        )

    low = lax.broadcasted_iota(jnp.int32, (32, 64), 1) < 32
    own_x = pl.ds(pl.multiple_of(view * 32, 32), 32)
    for z in range(8):
        a, b = final[0, :, z, :], final[1, :, z, :]
        turned = jnp.transpose(jnp.concatenate([b, a, a, b], axis=0))
        for half in range(2):
            at = 64 * half
            summed = jnp.where(low, turned[at : at + 32], turned[at + 32 : at + 64])
            out_ref[8 * half + z] = quarter[8 * half + z, own_x, :] * summed * 0.25


def local(estimate, measured, psf_taps, plane_source, plane_shift):
    dma = pltpu.SemaphoreType.DMA
    smem = pl.BlockSpec(memory_space=pltpu.SMEM)
    vmem = pl.BlockSpec(memory_space=pltpu.VMEM)
    hbm = pl.BlockSpec(memory_space=pl.ANY)
    out = pl.pallas_call(
        kernel,
        name="update",
        out_shape=jax.ShapeDtypeStruct((16, 32, 64), F32),
        in_specs=[smem, smem, vmem, hbm, hbm],
        out_specs=vmem,
        scratch_shapes=[
            pltpu.VMEM((16, 96, 128), F32),
            pltpu.VMEM((16, 64, 128), F32),
            pltpu.VMEM((2, 512, 128), F32),
            pltpu.VMEM((2, 512, 128), F32),
            pltpu.VMEM((2, 2, 256, 128), F32),
            pltpu.VMEM((2, 2, 256, 128), F32),
            pltpu.VMEM((2, 4, 16, 8, 128), F32),
            pltpu.VMEM((2, 4, 16, 8, 128), F32),
            pltpu.VMEM((32, 128), F32),
            pltpu.VMEM((4, 32, 128), F32),
            pltpu.VMEM((4, 32, 8, 128), F32),
            pltpu.VMEM((2, 3, 16, 8, 128), F32),
            pltpu.VMEM((2, 8, 8, 128), F32),
            pltpu.VMEM((2, 8, 8, 128), F32),
            pltpu.VMEM((2, 16, 8, 128), F32),
            pltpu.VMEM((16, 128, 64), F32),
            pltpu.VMEM((128, 128), F32),
            pltpu.VMEM((384, 128), B16),
            pltpu.VMEM((256, 768), B16),
            pltpu.VMEM((256, 768), B16),
            pltpu.VMEM((256, 512), B16),
            pltpu.VMEM((1536, 512), B16),
            dma((2,)), dma((2,)), dma((2,)), dma((4,)), dma((4,)),
            dma((2, 16)), dma((2, 16)), dma((2, 16)), dma((2, 16)),
            dma((2, 4, 16)), dma((2, 4, 16)), dma((2,)), dma((2,)),
            pltpu.SemaphoreType.REGULAR,
        ],
        compiler_params=pltpu.CompilerParams(
            collective_id=0, has_side_effects=True, vmem_limit_bytes=56 * 2**20
        ),
    )(jnp.transpose(psf_taps, (1, 0, 2)), plane_shift, plane_source, estimate, measured)
    return jnp.transpose(out, (0, 2, 1))


def solution(mesh):
    in_specs = (
        P("slab", "tile", None),
        P("view", "slab", "tile", None),
        P("view", None, None),
        P("view", None),
        P("view", None),
    )
    return jax.shard_map(
        local, mesh=mesh, in_specs=in_specs, out_specs=P("slab", "tile", "view"), check_vma=False
    )
```

```python
import jax
import jax.numpy as jnp
from jax import lax
from jax.experimental import pallas as pl
from jax.experimental.pallas import tpu as pltpu
from jax.sharding import PartitionSpec as P

MESH = pl.DeviceIdType.MESH
F32 = jnp.float32
B16 = jnp.bfloat16
TAPS = 31
RADIUS = 15
HALO = 16


def split(x):
    high = x.astype(B16)
    return high, (x - high.astype(F32)).astype(B16)


def left3(x):
    high, low = split(x)
    return jnp.concatenate([high, high, low], axis=1)


def right3(x):
    high, low = split(x)
    return jnp.concatenate([high, low, high], axis=0)


def dot(a, b):
    return jnp.dot(a, b, preferred_element_type=F32)


def circulant(taps, flip):
    total = taps[0]
    for t in range(1, TAPS):
        total = total + taps[t]
    row = lax.broadcasted_iota(jnp.int32, (128, 128), 0)
    col = lax.broadcasted_iota(jnp.int32, (128, 128), 1)
    off = lax.rem(col - row + RADIUS + 128, 128)
    out = jnp.zeros((128, 128), F32)
    for t in range(TAPS):
        out = jnp.where(off == t, taps[TAPS - 1 - t if flip else t], out)
    return out / jnp.full((128, 128), total)


def wide(block):
    row = lax.broadcasted_iota(jnp.int32, (128, 128), 0)
    col = lax.broadcasted_iota(jnp.int32, (128, 128), 1)
    near = jnp.abs(row - col) <= RADIUS
    a = jnp.where(near, block, 0.0)
    b = jnp.where(near, 0.0, block)
    return jnp.concatenate(
        [jnp.concatenate([a, b], axis=1), jnp.concatenate([b, a], axis=1)], axis=0
    )


ORDER = (1, 0, 3, 2)
FAR_FIRST = (10, 6, 14, 9, 11, 2, 8, 5, 7, 13, 15, 1, 3, 4, 12)


def kernel(
    taps_ref, shift_ref, source_ref, est_ref, meas_ref, out_ref,
    ext, meas, pack_m, pack_e, got_m, got_e, forth, seen, table, tables, coefs,
    final, edges, arrived, quarter, band_y, mix_x, band_z, natural, back_z, pick, back_x,
    local_sem, halo_send, halo_recv, tap_send, tap_recv, m_send, m_recv, e_send, e_recv,
    gauge, p_send, p_recv, edge_send, edge_recv, ready,
):
    slab, tile, view = lax.axis_index("slab"), lax.axis_index("tile"), lax.axis_index("view")
    side = 4
    sy, sx = slab // side, lax.rem(slab, side)
    up, down = lax.rem(tile + 1, 4), lax.rem(tile + 3, 4)

    def slab_at(d):
        dy, dx = d // side, lax.rem(d, side)
        return lax.rem(sy + dy, side) * side + lax.rem(sx + dx, side)

    def view_at(d):
        return lax.rem(view + d, 4)

    own_est = pltpu.make_async_copy(est_ref, ext.at[:, pl.ds(HALO, 64), :], local_sem.at[0])
    own_meas = pltpu.make_async_copy(meas_ref.at[0], meas, local_sem.at[1])
    own_est.start()
    own_meas.start()

    barrier = pltpu.get_barrier_semaphore()
    pl.semaphore_signal(barrier, inc=1, device_id=(slab, tile, view_at(2)), device_id_type=MESH)
    for d in FAR_FIRST:
        pl.semaphore_signal(
            barrier, inc=1, device_id=(slab_at(d), tile, view), device_id_type=MESH
        )
    for d in (1, 3):
        pl.semaphore_signal(
            barrier, inc=1, device_id=(slab, tile, view_at(d)), device_id_type=MESH
        )
    for t in (up, down):
        pl.semaphore_signal(barrier, inc=1, device_id=(slab, t, view), device_id_type=MESH)

    taps_z = [taps_ref[0, 0, t] for t in range(TAPS)]
    taps_y = [taps_ref[1, 0, t] for t in range(TAPS)]
    taps_x = [taps_ref[2, 0, t] for t in range(TAPS)]
    total_y = taps_y[0]
    for t in range(1, TAPS):
        total_y = total_y + taps_y[t]
    for t in range(TAPS):
        table[pl.ds(t, 1), :] = jnp.full((1, 128), taps_y[t])
    table[pl.ds(TAPS, 1), :] = jnp.zeros((1, 128), F32)
    table[...] = table[...] / jnp.full((32, 128), total_y)
    tables[view] = table[...]

    band_y[...] = circulant(taps_y, False)
    mix_x[...] = right3(circulant(taps_x, True))

    own_meas.wait()
    for j in range(16):
        amount = lax.rem(128 - shift_ref[0, slab * 16 + j], 128)
        plane = pltpu.roll(meas[j], amount, 1)
        for chunk, k in enumerate(ORDER):
            pack_m[chunk, pl.ds(j, 16, stride=16), :] = plane[16 * k : 16 * k + 16]

    def blur_rows(chunks, band, flat):
        by_y = dot(left3(band), right3(flat))
        tall = jnp.concatenate([by_y[:, 128 * z : 128 * z + 128] for z in range(16)], axis=0)
        by_x = dot(left3(tall), mix_x[...])
        for z in range(16):
            for i, chunk in enumerate(chunks):
                at = 32 * z + 16 * i
                pack_e[chunk, pl.ds(z, 16, stride=16), :] = by_x[at : at + 16, :]

    own_est.wait()
    blur_rows(
        (0, 3),
        band_y[32:64, 16:80],
        jnp.concatenate([ext[z, HALO : 64 + HALO, :] for z in range(16)], axis=1),
    )

    pl.semaphore_wait(barrier, 20)

    to_up = pltpu.make_async_remote_copy(
        src_ref=est_ref.at[:, pl.ds(64 - HALO, HALO), :], dst_ref=ext.at[:, pl.ds(0, HALO), :],
        send_sem=halo_send.at[0], recv_sem=halo_recv.at[0],
        device_id=(slab, up, view), device_id_type=MESH,
    )
    to_down = pltpu.make_async_remote_copy(
        src_ref=est_ref.at[:, pl.ds(0, HALO), :], dst_ref=ext.at[:, pl.ds(64 + HALO, HALO), :],
        send_sem=halo_send.at[1], recv_sem=halo_recv.at[1],
        device_id=(slab, down, view), device_id_type=MESH,
    )
    to_up.start()
    to_down.start()

    mine = pl.ds(pl.multiple_of(slab * 16, 16), 16)

    def exchange(chunk, pack, got, send, recv):
        def start(d, _):
            to = slab_at(d)
            pltpu.make_async_remote_copy(
                src_ref=pack.at[chunk, pl.ds(pl.multiple_of(to * 16, 16), 16), :],
                dst_ref=got.at[chunk, mine, :],
                send_sem=send.at[chunk], recv_sem=recv.at[chunk],
                device_id=(to, tile, view), device_id_type=MESH,
            ).start()
            return 0

        lax.fori_loop(1, 16, start, 0)
        got[chunk, mine, :] = pack[chunk, mine, :]

    def await_bytes(ref, sem):
        pltpu.make_async_copy(ref, ref, sem).wait()

    def exchange_m(chunk):
        exchange(chunk, pack_m, got_m, m_send, m_recv)

    def exchange_e(chunk):
        exchange(chunk, pack_e, got_e, e_send, e_recv)

    exchange_m(0)
    exchange_e(0)
    tap_copies = []
    for d in (2, 1, 3):
        c = pltpu.make_async_remote_copy(
            src_ref=table, dst_ref=tables.at[view],
            send_sem=tap_send.at[d], recv_sem=tap_recv.at[d],
            device_id=(slab, tile, view_at(d)), device_id_type=MESH,
        )
        c.start()
        tap_copies.append(c)
        pl.semaphore_signal(
            ready, inc=1, device_id=(slab, tile, view_at(d)), device_id_type=MESH
        )
    exchange_m(1)
    exchange_m(2)

    band_z[...] = left3(wide(circulant(taps_z, False)))
    natural[...] = wide(circulant(taps_z, True))
    for zq in range(4):
        rows = jnp.concatenate(
            [natural[16 * s + 4 * zq : 16 * s + 4 * zq + 4, :] for s in range(16)], axis=0
        )
        back_z[64 * zq : 64 * zq + 64, :] = left3(rows)
    plane_of = lax.broadcasted_iota(jnp.int32, (256, 256), 0)
    shown = jnp.where(jnp.broadcast_to(source_ref[...], (256, 256)) == plane_of, 1.0, 0.0)
    shown = shown.astype(B16)
    pick[...] = jnp.concatenate([shown, shown], axis=1)
    back_x[...] = right3(circulant(taps_x, False))
    final[...] = jnp.zeros_like(final)
    edges[...] = jnp.zeros_like(edges)

    to_up.wait()
    to_down.wait()
    blur_rows(
        (1, 2),
        jnp.concatenate([band_y[16:32, 0:96], band_y[64:80, 0:96]], axis=0),
        jnp.concatenate([ext[z] for z in range(16)], axis=1),
    )
    exchange_e(1)
    exchange_e(2)

    block = lax.broadcasted_iota(jnp.int32, (64, 128), 1) // 32
    half = pl.ds(pl.multiple_of(lax.rem(slab, 2) * 4, 4), 4)

    def process(chunk):
        await_bytes(got_m.at[chunk, pl.ds(0, 240)], m_recv.at[chunk])
        m_high, m_low = split(got_m[chunk])
        routed = dot(pick[...], jnp.concatenate([m_high, m_low], axis=0))
        await_bytes(got_e.at[chunk, pl.ds(0, 240)], e_recv.at[chunk])
        blurred = dot(band_z[...], right3(got_e[chunk]))
        pulled = dot(back_z[...], right3(routed / blurred))
        by_x = dot(left3(pulled), back_x[...])
        turned = [by_x] + [pltpu.roll(by_x, 32 * m, 1) for m in (1, 2, 3)]
        for w in range(4):
            out = turned[(3 - w) % 4][192:256]
            for zq in (2, 1, 0):
                out = jnp.where(block == zq, turned[(zq - w) % 4][64 * zq : 64 * zq + 64], out)
            forth[chunk, w] = out
        if chunk == 0:
            pl.semaphore_wait(ready, 3)

        def send(ds, dv):
            to, w = slab_at(ds), view_at(dv)
            pltpu.make_async_remote_copy(
                src_ref=forth.at[chunk, w, pl.ds(pl.multiple_of(to * 4, 4), 4), :],
                dst_ref=seen.at[chunk, view, slab // 2, half, :],
                send_sem=p_send.at[chunk, min(dv, 1)], recv_sem=p_recv.at[chunk, dv],
                device_id=(to, tile, w), device_id_type=MESH,
            ).start()

        def start(i, _):
            ds = lax.rem(i, 16)
            for dv in (2, 1, 3):
                send(ds, dv)
            return 0

        def start_own(ds, _):
            send(ds, 0)
            return 0

        lax.fori_loop(1, 17, start, 0)
        lax.fori_loop(1, 16, start_own, 0)
        seen[chunk, view, slab // 2, half, :] = forth[
            chunk, view, pl.ds(pl.multiple_of(slab * 4, 4), 4), :
        ]

    process(0)
    exchange_m(3)
    exchange_e(3)
    process(1)
    process(2)
    process(3)

    for c in tap_copies:
        c.wait()
    for v in range(4):
        for t in range(TAPS):
            coefs[v, t] = jnp.broadcast_to(tables[v, pl.ds(t, 1), :], (8, 128))
    for z in range(16):
        quarter[z] = jnp.transpose(ext[z, HALO : 64 + HALO, :])

    first = lax.broadcasted_iota(jnp.int32, (8, 128), 0) < 4

    def accumulate(chunk, dv):
        k = ORDER[chunk]
        v = lax.rem(view + 4 - dv, 4)
        if dv:
            await_bytes(seen.at[chunk, v], p_recv.at[chunk, dv])
        else:
            await_bytes(gauge, p_recv.at[chunk, dv])
        pairs = [seen[chunk, v, j] for j in range(8)]
        swapped = [pltpu.roll(p, 4, 0) for p in pairs]
        odd = [jnp.where(first, swapped[j], swapped[j + 1]) for j in range(7)]
        odd.append(jnp.where(first, swapped[7], 0.0))
        odd.append(jnp.where(first, 0.0, swapped[0]))
        lower = final.at[k - 1] if k else edges.at[0]
        upper = final.at[k + 1] if k < 3 else edges.at[1]
        for ref, kind in ((lower, 1), (upper, -1), (final.at[k], 0)):
            for j in range(8):
                total = None
                for d in range(-RADIUS, RADIUS + 1):
                    i, parity = j + d // 2 - 8 * kind, d % 2
                    if parity:
                        if not -1 <= i <= 7:
                            continue
                        data = odd[i]
                    else:
                        if not 0 <= i <= 7:
                            continue
                        data = pairs[i]
                    term = coefs[v, RADIUS - d] * data
                    total = term if total is None else total + term
                if total is not None:
                    ref[j] = ref[j] + total

    for chunk in range(3):
        for dv in (0, 2, 1, 3):
            accumulate(chunk, dv)
    edge_down = pltpu.make_async_remote_copy(
        src_ref=edges.at[0], dst_ref=arrived.at[0],
        send_sem=edge_send.at[0], recv_sem=edge_recv.at[0],
        device_id=(slab, down, view), device_id_type=MESH,
    )
    edge_up = pltpu.make_async_remote_copy(
        src_ref=edges.at[1], dst_ref=arrived.at[1],
        send_sem=edge_send.at[1], recv_sem=edge_recv.at[1],
        device_id=(slab, up, view), device_id_type=MESH,
    )
    edge_down.start()
    edge_up.start()
    for chunk in range(4):
        await_bytes(pack_m.at[chunk, pl.ds(0, 240)], m_send.at[chunk])
        await_bytes(pack_e.at[chunk, pl.ds(0, 240)], e_send.at[chunk])
        await_bytes(gauge, p_send.at[chunk, 0])
        await_bytes(forth.at[chunk, pl.ds(0, 3)], p_send.at[chunk, 1])
    for dv in (0, 2, 1, 3):
        accumulate(3, dv)
    edge_down.wait()
    edge_up.wait()
    final[3] = final[3] + arrived[0]
    final[0] = final[0] + arrived[1]

    own_x = pl.ds(pl.multiple_of(view * 32, 32), 32)
    rows = final.reshape(256, 128)
    for z in range(4):
        turned = jnp.transpose(rows[pl.ds(z, 64, stride=4), :])
        for zq in range(4):
            at = 4 * zq + z
            out_ref[at] = quarter[at, own_x, :] * turned[32 * zq : 32 * zq + 32] * 0.25


def local(estimate, measured, psf_taps, plane_source, plane_shift):
    dma = pltpu.SemaphoreType.DMA
    smem = pl.BlockSpec(memory_space=pltpu.SMEM)
    vmem = pl.BlockSpec(memory_space=pltpu.VMEM)
    hbm = pl.BlockSpec(memory_space=pl.ANY)
    out = pl.pallas_call(
        kernel,
        name="update",
        out_shape=jax.ShapeDtypeStruct((16, 32, 64), F32),
        in_specs=[smem, smem, vmem, hbm, hbm],
        out_specs=vmem,
        scratch_shapes=[
            pltpu.VMEM((16, 96, 128), F32),
            pltpu.VMEM((16, 64, 128), F32),
            pltpu.VMEM((4, 256, 128), F32),
            pltpu.VMEM((4, 256, 128), F32),
            pltpu.VMEM((4, 256, 128), F32),
            pltpu.VMEM((4, 256, 128), F32),
            pltpu.VMEM((4, 4, 64, 128), F32),
            pltpu.VMEM((4, 4, 8, 8, 128), F32),
            pltpu.VMEM((32, 128), F32),
            pltpu.VMEM((4, 32, 128), F32),
            pltpu.VMEM((4, 32, 8, 128), F32),
            pltpu.VMEM((4, 8, 8, 128), F32),
            pltpu.VMEM((2, 8, 8, 128), F32),
            pltpu.VMEM((2, 8, 8, 128), F32),
            pltpu.VMEM((16, 128, 64), F32),
            pltpu.VMEM((128, 128), F32),
            pltpu.VMEM((384, 128), B16),
            pltpu.VMEM((256, 768), B16),
            pltpu.VMEM((256, 256), F32),
            pltpu.VMEM((256, 768), B16),
            pltpu.VMEM((256, 512), B16),
            pltpu.VMEM((384, 128), B16),
            dma((2,)), dma((2,)), dma((2,)), dma((4,)), dma((4,)),
            dma((4,)), dma((4,)), dma((4,)), dma((4,)),
            pltpu.VMEM((15, 4, 128), F32),
            dma((4, 2)), dma((4, 4)), dma((2,)), dma((2,)),
            pltpu.SemaphoreType.REGULAR,
        ],
        compiler_params=pltpu.CompilerParams(
            collective_id=0, has_side_effects=True, vmem_limit_bytes=56 * 2**20
        ),
    )(jnp.transpose(psf_taps, (1, 0, 2)), plane_shift, plane_source, estimate, measured)
    return jnp.transpose(out, (0, 2, 1))


def solution(mesh):
    in_specs = (
        P("slab", "tile", None),
        P("view", "slab", "tile", None),
        P("view", None, None),
        P("view", None),
        P("view", None),
    )
    return jax.shard_map(
        local, mesh=mesh, in_specs=in_specs, out_specs=P("slab", "tile", "view"), check_vma=False
    )
```

```python
import jax
import jax.numpy as jnp
from jax import lax
from jax.experimental import pallas as pl
from jax.experimental.pallas import tpu as pltpu
from jax.sharding import PartitionSpec as P

MESH = pl.DeviceIdType.MESH
F32 = jnp.float32
B16 = jnp.bfloat16
TAPS = 31
RADIUS = 15
HALO = 16


def split(x):
    high = x.astype(B16)
    return high, (x - high.astype(F32)).astype(B16)


def left3(x):
    high, low = split(x)
    return jnp.concatenate([high, high, low], axis=1)


def right3(x):
    high, low = split(x)
    return jnp.concatenate([high, low, high], axis=0)


def dot(a, b):
    return jnp.dot(a, b, preferred_element_type=F32)


def circulant(taps, flip):
    total = taps[0]
    for t in range(1, TAPS):
        total = total + taps[t]
    row = lax.broadcasted_iota(jnp.int32, (8, 128), 0)
    col = lax.broadcasted_iota(jnp.int32, (8, 128), 1)
    off = lax.rem(col - row + RADIUS + 128, 128)
    top = jnp.zeros((8, 128), F32)
    for t in range(TAPS):
        top = jnp.where(off == t, taps[TAPS - 1 - t if flip else t], top)
    top = top / jnp.full((8, 128), total)
    return jnp.concatenate([top] + [pltpu.roll(top, 8 * b, 1) for b in range(1, 16)], axis=0)


def wide(block):
    row = lax.broadcasted_iota(jnp.int32, (128, 128), 0)
    col = lax.broadcasted_iota(jnp.int32, (128, 128), 1)
    near = jnp.abs(row - col) <= RADIUS
    a = jnp.where(near, block, 0.0)
    b = jnp.where(near, 0.0, block)
    return jnp.concatenate(
        [jnp.concatenate([a, b], axis=1), jnp.concatenate([b, a], axis=1)], axis=0
    )


ORDER = (1, 0, 3, 2)
M_SLOT = (0, 2, 3, 6)
E_SLOT = (1, 4, 5, 7)
RUNS = ((0, 2), (2, 4), (4, 5), (5, 6), (6, 8))
FAR_FIRST = (10, 6, 14, 9, 11, 2, 8, 5, 7, 13, 15, 1, 3, 4, 12)


def kernel(
    taps_hbm, shift_hbm, source_hbm, est_ref, meas_ref, out_ref,
    taps_ref, shift_ref, source_ref, ext, meas, pack, got, forth, seen, table, tables, coefs,
    final, edges, arrived, quarter, band_y, mix_x, band_z, natural, back_z, pick, back_x,
    local_sem, halo_send, halo_recv, tap_send, tap_recv, x_send, x_recv,
    gauge, p_send, p_recv, edge_send, edge_recv, ready,
):
    slab, tile, view = lax.axis_index("slab"), lax.axis_index("tile"), lax.axis_index("view")
    side = 4
    sy, sx = slab // side, lax.rem(slab, side)
    up, down = lax.rem(tile + 1, 4), lax.rem(tile + 3, 4)

    ys = [lax.rem(sy + d, side) * side for d in range(side)]
    xs = [lax.rem(sx + d, side) for d in range(side)]
    views = [lax.rem(view + d, 4) for d in range(4)]

    def slab_at(d):
        return ys[d // side] + xs[d % side]

    def view_at(d):
        return views[d]

    barrier = pltpu.get_barrier_semaphore()
    pl.semaphore_signal(barrier, inc=1, device_id=(slab, tile, view_at(2)), device_id_type=MESH)
    for d in FAR_FIRST:
        pl.semaphore_signal(
            barrier, inc=1, device_id=(slab_at(d), tile, view), device_id_type=MESH
        )
    for d in (1, 3):
        pl.semaphore_signal(
            barrier, inc=1, device_id=(slab, tile, view_at(d)), device_id_type=MESH
        )
    for t in (up, down):
        pl.semaphore_signal(barrier, inc=1, device_id=(slab, t, view), device_id_type=MESH)

    own_est = pltpu.make_async_copy(est_ref, ext.at[:, pl.ds(HALO, 64), :], local_sem.at[0])
    own_meas = pltpu.make_async_copy(meas_ref.at[0], meas, local_sem.at[1])
    own_taps = pltpu.make_async_copy(taps_hbm, taps_ref, local_sem.at[2])
    own_shift = pltpu.make_async_copy(shift_hbm, shift_ref, local_sem.at[3])
    own_source = pltpu.make_async_copy(source_hbm, source_ref, local_sem.at[4])
    for c in (own_taps, own_shift, own_meas, own_est, own_source):
        c.start()

    own_taps.wait()
    taps_z = [taps_ref[0, 0, t] for t in range(TAPS)]
    taps_y = [taps_ref[1, 0, t] for t in range(TAPS)]
    taps_x = [taps_ref[2, 0, t] for t in range(TAPS)]
    total_y = taps_y[0]
    for t in range(1, TAPS):
        total_y = total_y + taps_y[t]
    for t in range(TAPS):
        table[pl.ds(t, 1), :] = jnp.full((1, 128), taps_y[t])
    table[pl.ds(TAPS, 1), :] = jnp.zeros((1, 128), F32)
    table[...] = table[...] / jnp.full((32, 128), total_y)
    tables[view] = table[...]

    band_y[...] = circulant(taps_y, False)
    mix_x[...] = right3(circulant(taps_x, True))

    own_shift.wait()
    own_meas.wait()
    for j in range(16):
        amount = lax.rem(128 - shift_ref[0, slab * 16 + j], 128)
        plane = pltpu.roll(meas[j], amount, 1)
        for chunk, k in enumerate(ORDER):
            pack[M_SLOT[chunk], pl.ds(j, 16, stride=16), :] = plane[16 * k : 16 * k + 16]

    def blur_rows(chunks, band, flat):
        by_y = dot(left3(band), right3(flat))
        tall = jnp.concatenate([by_y[:, 128 * z : 128 * z + 128] for z in range(16)], axis=0)
        by_x = dot(left3(tall), mix_x[...])
        for z in range(16):
            for i, chunk in enumerate(chunks):
                at = 32 * z + 16 * i
                pack[E_SLOT[chunk], pl.ds(z, 16, stride=16), :] = by_x[at : at + 16, :]

    own_est.wait()
    blur_rows(
        (0, 3),
        band_y[32:64, 16:80],
        jnp.concatenate([ext[z, HALO : 64 + HALO, :] for z in range(16)], axis=1),
    )

    pl.semaphore_wait(barrier, 20)

    to_up = pltpu.make_async_remote_copy(
        src_ref=est_ref.at[:, pl.ds(64 - HALO, HALO), :], dst_ref=ext.at[:, pl.ds(0, HALO), :],
        send_sem=halo_send.at[0], recv_sem=halo_recv.at[0],
        device_id=(slab, up, view), device_id_type=MESH,
    )
    to_down = pltpu.make_async_remote_copy(
        src_ref=est_ref.at[:, pl.ds(0, HALO), :], dst_ref=ext.at[:, pl.ds(64 + HALO, HALO), :],
        send_sem=halo_send.at[1], recv_sem=halo_recv.at[1],
        device_id=(slab, down, view), device_id_type=MESH,
    )
    to_up.start()
    to_down.start()

    mine = pl.ds(pl.multiple_of(slab * 16, 16), 16)

    def exchange(run):
        lo, hi = RUNS[run]
        for d in FAR_FIRST:
            to = slab_at(d)
            pltpu.make_async_remote_copy(
                src_ref=pack.at[lo:hi, pl.ds(pl.multiple_of(to * 16, 16), 16), :],
                dst_ref=got.at[lo:hi, mine, :],
                send_sem=x_send.at[run], recv_sem=x_recv.at[run],
                device_id=(to, tile, view), device_id_type=MESH,
            ).start()
        for slot in range(lo, hi):
            got[slot, mine, :] = pack[slot, mine, :]

    def await_bytes(ref, sem):
        pltpu.make_async_copy(ref, ref, sem).wait()

    def await_run(run):
        lo, hi = RUNS[run]
        await_bytes(got.at[lo:hi, pl.ds(0, 240)], x_recv.at[run])

    exchange(0)
    tap_copies = []
    for d in (2, 1, 3):
        c = pltpu.make_async_remote_copy(
            src_ref=table, dst_ref=tables.at[view],
            send_sem=tap_send.at[d], recv_sem=tap_recv.at[d],
            device_id=(slab, tile, view_at(d)), device_id_type=MESH,
        )
        c.start()
        tap_copies.append(c)
        pl.semaphore_signal(
            ready, inc=1, device_id=(slab, tile, view_at(d)), device_id_type=MESH
        )
    exchange(1)

    band_z[...] = left3(wide(circulant(taps_z, False)))
    both = wide(circulant(taps_z, True))
    natural[0], natural[1] = both[:, 0:128], both[:, 128:256]
    for zq in range(4):
        rows = [natural[i, pl.ds(zq, 64, stride=4), :] for i in range(2)]
        back_z[64 * zq : 64 * zq + 64, :] = left3(jnp.concatenate(rows, axis=1))
    own_source.wait()
    plane_of = lax.broadcasted_iota(jnp.int32, (256, 256), 0)
    shown = jnp.where(jnp.broadcast_to(source_ref[...], (256, 256)) == plane_of, 1.0, 0.0)
    shown = shown.astype(B16)
    pick[...] = jnp.concatenate([shown, shown], axis=1)
    back_x[...] = right3(circulant(taps_x, False))
    final[...] = jnp.zeros_like(final)
    edges[...] = jnp.zeros_like(edges)

    to_up.wait()
    to_down.wait()
    blur_rows(
        (1, 2),
        jnp.concatenate([band_y[16:32, 0:96], band_y[64:80, 0:96]], axis=0),
        jnp.concatenate([ext[z] for z in range(16)], axis=1),
    )
    exchange(2)
    exchange(3)

    block = lax.broadcasted_iota(jnp.int32, (64, 128), 1) // 32
    half = pl.ds(pl.multiple_of(lax.rem(slab, 2) * 4, 4), 4)

    def process(chunk):
        for run in ((0,), (1, 2), (3,), (4,))[chunk]:
            await_run(run)
        m_high, m_low = split(got[M_SLOT[chunk]])
        routed = dot(pick[...], jnp.concatenate([m_high, m_low], axis=0))
        blurred = dot(band_z[...], right3(got[E_SLOT[chunk]]))
        pulled = dot(back_z[...], right3(routed / blurred))
        by_x = dot(left3(pulled), back_x[...])
        turned = [by_x] + [pltpu.roll(by_x, 32 * m, 1) for m in (1, 2, 3)]
        for w in range(4):
            out = turned[(3 - w) % 4][192:256]
            for zq in (2, 1, 0):
                out = jnp.where(block == zq, turned[(zq - w) % 4][64 * zq : 64 * zq + 64], out)
            forth[chunk, w] = out
        if chunk == 0:
            pl.semaphore_wait(ready, 3)

        def send(ds, dv):
            to, w = slab_at(ds), view_at(dv)
            pltpu.make_async_remote_copy(
                src_ref=forth.at[chunk, w, pl.ds(pl.multiple_of(to * 4, 4), 4), :],
                dst_ref=seen.at[chunk, view, slab // 2, half, :],
                send_sem=p_send.at[chunk, min(dv, 1)], recv_sem=p_recv.at[chunk, dv],
                device_id=(to, tile, w), device_id_type=MESH,
            ).start()

        for ds in FAR_FIRST:
            for dv in (2, 1, 3, 0):
                send(ds, dv)
        for dv in (2, 1, 3):
            send(0, dv)
        seen[chunk, view, slab // 2, half, :] = forth[
            chunk, view, pl.ds(pl.multiple_of(slab * 4, 4), 4), :
        ]

    process(0)
    exchange(4)
    process(1)
    process(2)
    process(3)

    for c in tap_copies:
        c.wait()
    for v in range(4):
        for t in range(TAPS):
            coefs[v, t] = jnp.broadcast_to(tables[v, pl.ds(t, 1), :], (8, 128))
    for z in range(16):
        quarter[z] = jnp.transpose(ext[z, HALO : 64 + HALO, :])

    first = lax.broadcasted_iota(jnp.int32, (8, 128), 0) < 4

    def accumulate(chunk, dv):
        k = ORDER[chunk]
        v = lax.rem(view + 4 - dv, 4)
        if dv:
            await_bytes(seen.at[chunk, v], p_recv.at[chunk, dv])
        else:
            await_bytes(gauge, p_recv.at[chunk, dv])
        pairs = [seen[chunk, v, j] for j in range(8)]
        swapped = [pltpu.roll(p, 4, 0) for p in pairs]
        odd = [jnp.where(first, swapped[j], swapped[j + 1]) for j in range(7)]
        odd.append(jnp.where(first, swapped[7], 0.0))
        odd.append(jnp.where(first, 0.0, swapped[0]))
        lower = final.at[k - 1] if k else edges.at[0]
        upper = final.at[k + 1] if k < 3 else edges.at[1]
        for ref, kind in ((lower, 1), (upper, -1), (final.at[k], 0)):
            for j in range(8):
                total = None
                for d in range(-RADIUS, RADIUS + 1):
                    i, parity = j + d // 2 - 8 * kind, d % 2
                    if parity:
                        if not -1 <= i <= 7:
                            continue
                        data = odd[i]
                    else:
                        if not 0 <= i <= 7:
                            continue
                        data = pairs[i]
                    term = coefs[v, RADIUS - d] * data
                    total = term if total is None else total + term
                if total is not None:
                    ref[j] = ref[j] + total

    for chunk in range(3):
        for dv in (0, 2, 1, 3):
            accumulate(chunk, dv)
    edge_down = pltpu.make_async_remote_copy(
        src_ref=edges.at[0], dst_ref=arrived.at[0],
        send_sem=edge_send.at[0], recv_sem=edge_recv.at[0],
        device_id=(slab, down, view), device_id_type=MESH,
    )
    edge_up = pltpu.make_async_remote_copy(
        src_ref=edges.at[1], dst_ref=arrived.at[1],
        send_sem=edge_send.at[1], recv_sem=edge_recv.at[1],
        device_id=(slab, up, view), device_id_type=MESH,
    )
    edge_down.start()
    edge_up.start()
    for chunk in range(4):
        await_bytes(gauge, p_send.at[chunk, 0])
        await_bytes(forth.at[chunk, pl.ds(0, 3)], p_send.at[chunk, 1])
    for run, (lo, hi) in enumerate(RUNS):
        await_bytes(pack.at[lo:hi, pl.ds(0, 240)], x_send.at[run])
    for dv in (0, 2, 1, 3):
        accumulate(3, dv)
    edge_down.wait()
    edge_up.wait()
    final[3] = final[3] + arrived[0]
    final[0] = final[0] + arrived[1]

    own_x = pl.ds(pl.multiple_of(view * 32, 32), 32)
    rows = final.reshape(256, 128)
    for z in range(4):
        turned = jnp.transpose(rows[pl.ds(z, 64, stride=4), :])
        for zq in range(4):
            at = 4 * z + zq
            out_ref[at] = quarter[at, own_x, :] * turned[32 * zq : 32 * zq + 32] * 0.25


def local(estimate, measured, psf_taps, plane_source, plane_shift):
    dma = pltpu.SemaphoreType.DMA
    vmem = pl.BlockSpec(memory_space=pltpu.VMEM)
    hbm = pl.BlockSpec(memory_space=pl.ANY)
    out = pl.pallas_call(
        kernel,
        name="update",
        out_shape=pltpu.VMEM((16, 32, 64), F32),
        in_specs=[hbm] * 5,
        out_specs=vmem,
        scratch_shapes=[
            pltpu.SMEM((3, 1, TAPS), F32),
            pltpu.SMEM((1, 256), jnp.int32),
            pltpu.VMEM((1, 256), jnp.int32),
            pltpu.VMEM((16, 96, 128), F32),
            pltpu.VMEM((16, 64, 128), F32),
            pltpu.VMEM((8, 256, 128), F32),
            pltpu.VMEM((8, 256, 128), F32),
            pltpu.VMEM((4, 4, 64, 128), F32),
            pltpu.VMEM((4, 4, 8, 8, 128), F32),
            pltpu.VMEM((32, 128), F32),
            pltpu.VMEM((4, 32, 128), F32),
            pltpu.VMEM((4, 32, 8, 128), F32),
            pltpu.VMEM((4, 8, 8, 128), F32),
            pltpu.VMEM((2, 8, 8, 128), F32),
            pltpu.VMEM((2, 8, 8, 128), F32),
            pltpu.VMEM((16, 128, 64), F32),
            pltpu.VMEM((128, 128), F32),
            pltpu.VMEM((384, 128), B16),
            pltpu.VMEM((256, 768), B16),
            pltpu.VMEM((2, 256, 128), F32),
            pltpu.VMEM((256, 768), B16),
            pltpu.VMEM((256, 512), B16),
            pltpu.VMEM((384, 128), B16),
            dma((5,)), dma((2,)), dma((2,)), dma((4,)), dma((4,)),
            dma((5,)), dma((5,)),
            pltpu.VMEM((15, 4, 128), F32),
            dma((4, 2)), dma((4, 4)), dma((2,)), dma((2,)),
            pltpu.SemaphoreType.REGULAR,
        ],
        compiler_params=pltpu.CompilerParams(
            collective_id=0, has_side_effects=True, vmem_limit_bytes=56 * 2**20
        ),
    )(jnp.transpose(psf_taps, (1, 0, 2)), plane_shift, plane_source, estimate, measured)
    return jnp.transpose(out, (0, 2, 1))


def solution(mesh):
    in_specs = (
        P("slab", "tile", None),
        P("view", "slab", "tile", None),
        P("view", None, None),
        P("view", None),
        P("view", None),
    )
    return jax.shard_map(
        local, mesh=mesh, in_specs=in_specs, out_specs=P("slab", "tile", "view"), check_vma=False
    )
```

```python
import jax
import jax.numpy as jnp
from jax import lax
from jax.experimental import pallas as pl
from jax.experimental.pallas import tpu as pltpu
from jax.sharding import PartitionSpec as P

MESH = pl.DeviceIdType.MESH
F32 = jnp.float32
B16 = jnp.bfloat16
TAPS = 31
RADIUS = 15
HALO = 16


def split(x):
    high = x.astype(B16)
    return high, (x - high.astype(F32)).astype(B16)


def left3(x):
    high, low = split(x)
    return jnp.concatenate([high, high, low], axis=1)


def right3(x):
    high, low = split(x)
    return jnp.concatenate([high, low, high], axis=0)


def dot(a, b):
    return jnp.dot(a, b, preferred_element_type=F32)


def circulant(taps, flip):
    total = taps[0]
    for t in range(1, TAPS):
        total = total + taps[t]
    row = lax.broadcasted_iota(jnp.int32, (8, 128), 0)
    col = lax.broadcasted_iota(jnp.int32, (8, 128), 1)
    off = lax.rem(col - row + RADIUS + 128, 128)
    top = jnp.zeros((8, 128), F32)
    for t in range(TAPS):
        top = jnp.where(off == t, taps[TAPS - 1 - t if flip else t], top)
    top = top / jnp.full((8, 128), total)
    return jnp.concatenate([top] + [pltpu.roll(top, 8 * b, 1) for b in range(1, 16)], axis=0)


def wide(block):
    row = lax.broadcasted_iota(jnp.int32, (128, 128), 0)
    col = lax.broadcasted_iota(jnp.int32, (128, 128), 1)
    near = jnp.abs(row - col) <= RADIUS
    a = jnp.where(near, block, 0.0)
    b = jnp.where(near, 0.0, block)
    return jnp.concatenate(
        [jnp.concatenate([a, b], axis=1), jnp.concatenate([b, a], axis=1)], axis=0
    )


ORDER = (1, 0, 3, 2)
M_SLOT = (0, 2, 3, 6)
E_SLOT = (1, 4, 5, 7)
RUNS = ((0, 2), (2, 4), (4, 5), (5, 6), (6, 8))
FAR_FIRST = (10, 6, 14, 9, 11, 2, 8, 5, 7, 13, 15, 1, 3, 4, 12)


def kernel(
    taps_hbm, shift_hbm, source_hbm, est_ref, meas_ref, out_ref,
    taps_ref, shift_ref, source_ref, ext, meas, pack, got, forth, seen, table, tables, coefs,
    final, edges, arrived, quarter, band_y, mix_x, band_z, natural, back_z, pick, back_x,
    local_sem, halo_send, halo_recv, tap_send, tap_recv, x_send, x_recv,
    gauge, p_send, p_recv, edge_send, edge_recv, ready,
):
    slab, tile, view = lax.axis_index("slab"), lax.axis_index("tile"), lax.axis_index("view")
    side = 4
    sy, sx = slab // side, lax.rem(slab, side)
    up, down = lax.rem(tile + 1, 4), lax.rem(tile + 3, 4)

    ys = [lax.rem(sy + d, side) * side for d in range(side)]
    xs = [lax.rem(sx + d, side) for d in range(side)]
    views = [lax.rem(view + d, 4) for d in range(4)]

    def slab_at(d):
        return ys[d // side] + xs[d % side]

    def view_at(d):
        return views[d]

    barrier = pltpu.get_barrier_semaphore()
    pl.semaphore_signal(barrier, inc=1, device_id=(slab, tile, view_at(2)), device_id_type=MESH)
    for d in FAR_FIRST:
        pl.semaphore_signal(
            barrier, inc=1, device_id=(slab_at(d), tile, view), device_id_type=MESH
        )
    for d in (1, 3):
        pl.semaphore_signal(
            barrier, inc=1, device_id=(slab, tile, view_at(d)), device_id_type=MESH
        )
    for t in (up, down):
        pl.semaphore_signal(barrier, inc=1, device_id=(slab, t, view), device_id_type=MESH)

    own_est = pltpu.make_async_copy(est_ref, ext.at[:, pl.ds(HALO, 64), :], local_sem.at[0])
    own_meas = pltpu.make_async_copy(meas_ref.at[0], meas, local_sem.at[1])
    own_taps = pltpu.make_async_copy(taps_hbm, taps_ref, local_sem.at[2])
    own_shift = pltpu.make_async_copy(shift_hbm, shift_ref, local_sem.at[3])
    own_source = pltpu.make_async_copy(source_hbm, source_ref, local_sem.at[4])
    for c in (own_taps, own_shift, own_meas, own_est, own_source):
        c.start()

    own_taps.wait()
    taps_z = [taps_ref[0, 0, t] for t in range(TAPS)]
    taps_y = [taps_ref[1, 0, t] for t in range(TAPS)]
    taps_x = [taps_ref[2, 0, t] for t in range(TAPS)]
    total_y = taps_y[0]
    for t in range(1, TAPS):
        total_y = total_y + taps_y[t]
    for t in range(TAPS):
        table[pl.ds(t, 1), :] = jnp.full((1, 128), taps_y[t])
    table[pl.ds(TAPS, 1), :] = jnp.zeros((1, 128), F32)
    table[...] = table[...] / jnp.full((32, 128), total_y)
    tables[view] = table[...]

    band_y[...] = circulant(taps_y, False)
    mix_x[...] = right3(circulant(taps_x, True))

    own_shift.wait()
    own_meas.wait()
    for j in range(16):
        amount = lax.rem(128 - shift_ref[0, slab * 16 + j], 128)
        plane = pltpu.roll(meas[j], amount, 1)
        for chunk, k in enumerate(ORDER):
            pack[M_SLOT[chunk], pl.ds(j, 16, stride=16), :] = plane[16 * k : 16 * k + 16]

    def blur_rows(chunks, band, flat):
        by_y = dot(left3(band), right3(flat))
        tall = jnp.concatenate([by_y[:, 128 * z : 128 * z + 128] for z in range(16)], axis=0)
        by_x = dot(left3(tall), mix_x[...])
        for z in range(16):
            for i, chunk in enumerate(chunks):
                at = 32 * z + 16 * i
                pack[E_SLOT[chunk], pl.ds(z, 16, stride=16), :] = by_x[at : at + 16, :]

    own_est.wait()
    blur_rows(
        (0, 3),
        band_y[32:64, 16:80],
        jnp.concatenate([ext[z, HALO : 64 + HALO, :] for z in range(16)], axis=1),
    )

    pl.semaphore_wait(barrier, 20)

    to_up = pltpu.make_async_remote_copy(
        src_ref=est_ref.at[:, pl.ds(64 - HALO, HALO), :], dst_ref=ext.at[:, pl.ds(0, HALO), :],
        send_sem=halo_send.at[0], recv_sem=halo_recv.at[0],
        device_id=(slab, up, view), device_id_type=MESH,
    )
    to_down = pltpu.make_async_remote_copy(
        src_ref=est_ref.at[:, pl.ds(0, HALO), :], dst_ref=ext.at[:, pl.ds(64 + HALO, HALO), :],
        send_sem=halo_send.at[1], recv_sem=halo_recv.at[1],
        device_id=(slab, down, view), device_id_type=MESH,
    )
    to_up.start()
    to_down.start()

    mine = pl.ds(pl.multiple_of(slab * 16, 16), 16)

    def exchange(run):
        lo, hi = RUNS[run]

        def send(to):
            pltpu.make_async_remote_copy(
                src_ref=pack.at[lo:hi, pl.ds(pl.multiple_of(to * 16, 16), 16), :],
                dst_ref=got.at[lo:hi, mine, :],
                send_sem=x_send.at[run], recv_sem=x_recv.at[run],
                device_id=(to, tile, view), device_id_type=MESH,
            ).start()

        def start(dy, _):
            row = lax.rem(sy + dy, side) * side
            for dx in (2, 1, 3, 0):
                send(row + xs[dx])
            return 0

        lax.fori_loop(1, side, start, 0)
        for dx in (2, 1, 3):
            send(ys[0] + xs[dx])
        for slot in range(lo, hi):
            got[slot, mine, :] = pack[slot, mine, :]

    def await_bytes(ref, sem):
        pltpu.make_async_copy(ref, ref, sem).wait()

    def await_run(run):
        lo, hi = RUNS[run]
        await_bytes(got.at[lo:hi, pl.ds(0, 240)], x_recv.at[run])

    exchange(0)
    tap_copies = []
    for d in (2, 1, 3):
        c = pltpu.make_async_remote_copy(
            src_ref=table, dst_ref=tables.at[view],
            send_sem=tap_send.at[d], recv_sem=tap_recv.at[d],
            device_id=(slab, tile, view_at(d)), device_id_type=MESH,
        )
        c.start()
        tap_copies.append(c)
        pl.semaphore_signal(
            ready, inc=1, device_id=(slab, tile, view_at(d)), device_id_type=MESH
        )
    exchange(1)

    band_z[...] = left3(wide(circulant(taps_z, False)))
    both = wide(circulant(taps_z, True))
    natural[0], natural[1] = both[:, 0:128], both[:, 128:256]
    for zq in range(4):
        rows = [natural[i, pl.ds(zq, 64, stride=4), :] for i in range(2)]
        back_z[64 * zq : 64 * zq + 64, :] = left3(jnp.concatenate(rows, axis=1))
    own_source.wait()
    plane_of = lax.broadcasted_iota(jnp.int32, (256, 256), 0)
    shown = jnp.where(jnp.broadcast_to(source_ref[...], (256, 256)) == plane_of, 1.0, 0.0)
    shown = shown.astype(B16)
    pick[...] = jnp.concatenate([shown, shown], axis=1)
    back_x[...] = right3(circulant(taps_x, False))
    final[...] = jnp.zeros_like(final)
    edges[...] = jnp.zeros_like(edges)

    to_up.wait()
    to_down.wait()
    blur_rows(
        (1, 2),
        jnp.concatenate([band_y[16:32, 0:96], band_y[64:80, 0:96]], axis=0),
        jnp.concatenate([ext[z] for z in range(16)], axis=1),
    )
    exchange(2)
    exchange(3)

    block = lax.broadcasted_iota(jnp.int32, (64, 128), 1) // 32
    half = pl.ds(pl.multiple_of(lax.rem(slab, 2) * 4, 4), 4)

    def process(chunk):
        for run in ((0,), (1, 2), (3,), (4,))[chunk]:
            await_run(run)
        m_high, m_low = split(got[M_SLOT[chunk]])
        routed = dot(pick[...], jnp.concatenate([m_high, m_low], axis=0))
        blurred = dot(band_z[...], right3(got[E_SLOT[chunk]]))
        pulled = dot(back_z[...], right3(routed / blurred))
        by_x = dot(left3(pulled), back_x[...])
        turned = [by_x] + [pltpu.roll(by_x, 32 * m, 1) for m in (1, 2, 3)]
        for w in range(4):
            out = turned[(3 - w) % 4][192:256]
            for zq in (2, 1, 0):
                out = jnp.where(block == zq, turned[(zq - w) % 4][64 * zq : 64 * zq + 64], out)
            forth[chunk, w] = out
        seen[chunk, view, slab // 2, half, :] = forth[
            chunk, view, pl.ds(pl.multiple_of(slab * 4, 4), 4), :
        ]

    def send_quarter(chunk, w):
        dv = lax.rem(w - view + 4, 4)

        def send(to, sem):
            pltpu.make_async_remote_copy(
                src_ref=forth.at[chunk, w, pl.ds(pl.multiple_of(to * 4, 4), 4), :],
                dst_ref=seen.at[chunk, view, slab // 2, half, :],
                send_sem=p_send.at[chunk, sem], recv_sem=p_recv.at[chunk, dv],
                device_id=(to, tile, w), device_id_type=MESH,
            ).start()

        def start(dy, _):
            row = lax.rem(sy + dy, side) * side
            for dx in (2, 1, 3, 0):
                send(row + xs[dx], 0)
            return 0

        lax.fori_loop(1, side, start, 0)
        for dx in (2, 1, 3):
            send(ys[0] + xs[dx], 0)

        @pl.when(w != view)
        def _():
            send(slab, 1)

    process(0)
    pl.semaphore_wait(ready, 3)
    for w in (0, 1, 2, 3):
        send_quarter(0, w)
    exchange(4)
    process(1)
    for w in (0, 1, 2, 3):
        send_quarter(1, w)
    process(2)
    for w in (0, 1, 2, 3):
        send_quarter(2, w)
    process(3)
    for w in (0, 1, 2, 3):
        send_quarter(3, w)
    for c in tap_copies:
        c.wait()
    for v in range(4):
        for t in range(TAPS):
            coefs[v, t] = jnp.broadcast_to(tables[v, pl.ds(t, 1), :], (8, 128))
    for z in range(16):
        quarter[z] = jnp.transpose(ext[z, HALO : 64 + HALO, :])

    first = lax.broadcasted_iota(jnp.int32, (8, 128), 0) < 4

    def accumulate(chunk, dv):
        k = ORDER[chunk]
        v = lax.rem(view + 4 - dv, 4)
        if dv:
            await_bytes(seen.at[chunk, v], p_recv.at[chunk, dv])
        else:
            await_bytes(gauge, p_recv.at[chunk, dv])
        pairs = [seen[chunk, v, j] for j in range(8)]
        swapped = [pltpu.roll(p, 4, 0) for p in pairs]
        odd = [jnp.where(first, swapped[j], swapped[j + 1]) for j in range(7)]
        odd.append(jnp.where(first, swapped[7], 0.0))
        odd.append(jnp.where(first, 0.0, swapped[0]))
        lower = final.at[k - 1] if k else edges.at[0]
        upper = final.at[k + 1] if k < 3 else edges.at[1]
        for ref, kind in ((lower, 1), (upper, -1), (final.at[k], 0)):
            for j in range(8):
                total = None
                for d in range(-RADIUS, RADIUS + 1):
                    i, parity = j + d // 2 - 8 * kind, d % 2
                    if parity:
                        if not -1 <= i <= 7:
                            continue
                        data = odd[i]
                    else:
                        if not 0 <= i <= 7:
                            continue
                        data = pairs[i]
                    term = coefs[v, RADIUS - d] * data
                    total = term if total is None else total + term
                if total is not None:
                    ref[j] = ref[j] + total

    for chunk in range(3):
        for dv in (0, 2, 1, 3):
            accumulate(chunk, dv)
    edge_down = pltpu.make_async_remote_copy(
        src_ref=edges.at[0], dst_ref=arrived.at[0],
        send_sem=edge_send.at[0], recv_sem=edge_recv.at[0],
        device_id=(slab, down, view), device_id_type=MESH,
    )
    edge_up = pltpu.make_async_remote_copy(
        src_ref=edges.at[1], dst_ref=arrived.at[1],
        send_sem=edge_send.at[1], recv_sem=edge_recv.at[1],
        device_id=(slab, up, view), device_id_type=MESH,
    )
    edge_down.start()
    edge_up.start()
    for dv in (0, 2, 1, 3):
        accumulate(3, dv)
    edge_down.wait()
    edge_up.wait()
    final[3] = final[3] + arrived[0]
    final[0] = final[0] + arrived[1]

    own_x = pl.ds(pl.multiple_of(view * 32, 32), 32)
    rows = final.reshape(256, 128)
    for z in range(4):
        turned = jnp.transpose(rows[pl.ds(z, 64, stride=4), :])
        for zq in range(4):
            at = 4 * z + zq
            out_ref[at] = quarter[at, own_x, :] * turned[32 * zq : 32 * zq + 32] * 0.25
    for chunk in range(4):
        await_bytes(got.at[0, pl.ds(0, 240)], p_send.at[chunk, 0])
        await_bytes(gauge.at[pl.ds(0, 3)], p_send.at[chunk, 1])
    for run, (lo, hi) in enumerate(RUNS):
        await_bytes(pack.at[lo:hi, pl.ds(0, 240)], x_send.at[run])


def local(estimate, measured, psf_taps, plane_source, plane_shift):
    dma = pltpu.SemaphoreType.DMA
    vmem = pl.BlockSpec(memory_space=pltpu.VMEM)
    hbm = pl.BlockSpec(memory_space=pl.ANY)
    out = pl.pallas_call(
        kernel,
        name="update",
        out_shape=pltpu.VMEM((16, 32, 64), F32),
        in_specs=[hbm] * 5,
        out_specs=vmem,
        scratch_shapes=[
            pltpu.SMEM((3, 1, TAPS), F32),
            pltpu.SMEM((1, 256), jnp.int32),
            pltpu.VMEM((1, 256), jnp.int32),
            pltpu.VMEM((16, 96, 128), F32),
            pltpu.VMEM((16, 64, 128), F32),
            pltpu.VMEM((8, 256, 128), F32),
            pltpu.VMEM((8, 256, 128), F32),
            pltpu.VMEM((4, 4, 64, 128), F32),
            pltpu.VMEM((4, 4, 8, 8, 128), F32),
            pltpu.VMEM((32, 128), F32),
            pltpu.VMEM((4, 32, 128), F32),
            pltpu.VMEM((4, 32, 8, 128), F32),
            pltpu.VMEM((4, 8, 8, 128), F32),
            pltpu.VMEM((2, 8, 8, 128), F32),
            pltpu.VMEM((2, 8, 8, 128), F32),
            pltpu.VMEM((16, 128, 64), F32),
            pltpu.VMEM((128, 128), F32),
            pltpu.VMEM((384, 128), B16),
            pltpu.VMEM((256, 768), B16),
            pltpu.VMEM((2, 256, 128), F32),
            pltpu.VMEM((256, 768), B16),
            pltpu.VMEM((256, 512), B16),
            pltpu.VMEM((384, 128), B16),
            dma((5,)), dma((2,)), dma((2,)), dma((4,)), dma((4,)),
            dma((5,)), dma((5,)),
            pltpu.VMEM((15, 4, 128), F32),
            dma((4, 2)), dma((4, 4)), dma((2,)), dma((2,)),
            pltpu.SemaphoreType.REGULAR,
        ],
        compiler_params=pltpu.CompilerParams(
            collective_id=0, has_side_effects=True, vmem_limit_bytes=56 * 2**20
        ),
    )(jnp.transpose(psf_taps, (1, 0, 2)), plane_shift, plane_source, estimate, measured)
    return jnp.transpose(out, (0, 2, 1))


def solution(mesh):
    in_specs = (
        P("slab", "tile", None),
        P("view", "slab", "tile", None),
        P("view", None, None),
        P("view", None),
        P("view", None),
    )
    return jax.shard_map(
        local, mesh=mesh, in_specs=in_specs, out_specs=P("slab", "tile", "view"), check_vma=False
    )
```

```python
import jax
import jax.numpy as jnp
from jax import lax
from jax.experimental import pallas as pl
from jax.experimental.pallas import tpu as pltpu
from jax.sharding import PartitionSpec as P

MESH = pl.DeviceIdType.MESH
F32 = jnp.float32
B16 = jnp.bfloat16
TAPS = 31
RADIUS = 15
HALO = 16


def split(x):
    high = x.astype(B16)
    return high, (x - high.astype(F32)).astype(B16)


def left3(x):
    high, low = split(x)
    return jnp.concatenate([high, high, low], axis=1)


def right3(x):
    high, low = split(x)
    return jnp.concatenate([high, low, high], axis=0)


def dot(a, b):
    return jnp.dot(a, b, preferred_element_type=F32)


def circulant(taps, flip):
    total = taps[0]
    for t in range(1, TAPS):
        total = total + taps[t]
    row = lax.broadcasted_iota(jnp.int32, (8, 128), 0)
    col = lax.broadcasted_iota(jnp.int32, (8, 128), 1)
    off = lax.rem(col - row + RADIUS + 128, 128)
    top = jnp.zeros((8, 128), F32)
    for t in range(TAPS):
        top = jnp.where(off == t, taps[TAPS - 1 - t if flip else t], top)
    top = top / jnp.full((8, 128), total)
    return jnp.concatenate([top] + [pltpu.roll(top, 8 * b, 1) for b in range(1, 16)], axis=0)


def wide(block):
    row = lax.broadcasted_iota(jnp.int32, (128, 128), 0)
    col = lax.broadcasted_iota(jnp.int32, (128, 128), 1)
    near = jnp.abs(row - col) <= RADIUS
    a = jnp.where(near, block, 0.0)
    b = jnp.where(near, 0.0, block)
    return jnp.concatenate(
        [jnp.concatenate([a, b], axis=1), jnp.concatenate([b, a], axis=1)], axis=0
    )


ORDER = (1, 0, 3, 2)
M_SLOT = (0, 2, 3, 6)
E_SLOT = (1, 4, 5, 7)
RUNS = ((0, 2), (2, 4), (4, 5), (5, 6), (6, 8))
FAR_FIRST = (10, 6, 14, 9, 11, 2, 8, 5, 7, 13, 15, 1, 3, 4, 12)


def kernel(
    taps_hbm, shift_hbm, source_hbm, est_ref, meas_ref, out_ref,
    taps_ref, shift_ref, source_ref, ext, meas, pack, got, forth, seen, table, tables, coefs,
    final, edges, arrived, quarter, band_y, mix_x, band_z, natural, back_z, pick, back_x,
    local_sem, halo_send, halo_recv, tap_send, tap_recv, x_send, x_recv,
    gauge, p_send, p_recv, edge_send, edge_recv, ready,
):
    slab, tile, view = lax.axis_index("slab"), lax.axis_index("tile"), lax.axis_index("view")
    side = 4
    sy, sx = slab // side, lax.rem(slab, side)
    up, down = lax.rem(tile + 1, 4), lax.rem(tile + 3, 4)

    ys = [lax.rem(sy + d, side) * side for d in range(side)]
    xs = [lax.rem(sx + d, side) for d in range(side)]
    views = [lax.rem(view + d, 4) for d in range(4)]

    def slab_at(d):
        return ys[d // side] + xs[d % side]

    def view_at(d):
        return views[d]

    barrier = pltpu.get_barrier_semaphore()
    pl.semaphore_signal(barrier, inc=1, device_id=(slab, tile, view_at(2)), device_id_type=MESH)
    for d in FAR_FIRST:
        pl.semaphore_signal(
            barrier, inc=1, device_id=(slab_at(d), tile, view), device_id_type=MESH
        )
    for d in (1, 3):
        pl.semaphore_signal(
            barrier, inc=1, device_id=(slab, tile, view_at(d)), device_id_type=MESH
        )
    for t in (up, down):
        pl.semaphore_signal(barrier, inc=1, device_id=(slab, t, view), device_id_type=MESH)

    own_est = pltpu.make_async_copy(est_ref, ext.at[:, pl.ds(HALO, 64), :], local_sem.at[0])
    own_meas = pltpu.make_async_copy(meas_ref.at[0], meas, local_sem.at[1])
    own_taps = pltpu.make_async_copy(taps_hbm, taps_ref, local_sem.at[2])
    own_shift = pltpu.make_async_copy(shift_hbm, shift_ref, local_sem.at[3])
    own_source = pltpu.make_async_copy(source_hbm, source_ref, local_sem.at[4])
    for c in (own_taps, own_shift, own_meas, own_est, own_source):
        c.start()

    own_taps.wait()
    taps_z = [taps_ref[0, 0, t] for t in range(TAPS)]
    taps_y = [taps_ref[1, 0, t] for t in range(TAPS)]
    taps_x = [taps_ref[2, 0, t] for t in range(TAPS)]
    total_y = taps_y[0]
    for t in range(1, TAPS):
        total_y = total_y + taps_y[t]
    for t in range(TAPS):
        table[pl.ds(t, 1), :] = jnp.full((1, 128), taps_y[t])
    table[pl.ds(TAPS, 1), :] = jnp.zeros((1, 128), F32)
    table[...] = table[...] / jnp.full((32, 128), total_y)
    tables[view] = table[...]

    band_y[...] = circulant(taps_y, False)
    mix_x[...] = right3(circulant(taps_x, True))

    own_shift.wait()
    own_meas.wait()
    for j in range(16):
        amount = lax.rem(128 - shift_ref[0, slab * 16 + j], 128)
        plane = pltpu.roll(meas[j], amount, 1)
        for chunk, k in enumerate(ORDER):
            pack[M_SLOT[chunk], pl.ds(j, 16, stride=16), :] = plane[16 * k : 16 * k + 16]

    def blur_rows(chunks, band, flat):
        by_y = dot(left3(band), right3(flat))
        tall = jnp.concatenate([by_y[:, 128 * z : 128 * z + 128] for z in range(16)], axis=0)
        by_x = dot(left3(tall), mix_x[...])
        for z in range(16):
            for i, chunk in enumerate(chunks):
                at = 32 * z + 16 * i
                pack[E_SLOT[chunk], pl.ds(z, 16, stride=16), :] = by_x[at : at + 16, :]

    own_est.wait()
    blur_rows(
        (0, 3),
        band_y[32:64, 16:80],
        jnp.concatenate([ext[z, HALO : 64 + HALO, :] for z in range(16)], axis=1),
    )

    pl.semaphore_wait(barrier, 20)

    to_up = pltpu.make_async_remote_copy(
        src_ref=est_ref.at[:, pl.ds(64 - HALO, HALO), :], dst_ref=ext.at[:, pl.ds(0, HALO), :],
        send_sem=halo_send.at[0], recv_sem=halo_recv.at[0],
        device_id=(slab, up, view), device_id_type=MESH,
    )
    to_down = pltpu.make_async_remote_copy(
        src_ref=est_ref.at[:, pl.ds(0, HALO), :], dst_ref=ext.at[:, pl.ds(64 + HALO, HALO), :],
        send_sem=halo_send.at[1], recv_sem=halo_recv.at[1],
        device_id=(slab, down, view), device_id_type=MESH,
    )
    to_up.start()
    to_down.start()

    mine = pl.ds(pl.multiple_of(slab * 16, 16), 16)

    def exchange(run):
        lo, hi = RUNS[run]

        def send(to):
            pltpu.make_async_remote_copy(
                src_ref=pack.at[lo:hi, pl.ds(pl.multiple_of(to * 16, 16), 16), :],
                dst_ref=got.at[lo:hi, mine, :],
                send_sem=x_send.at[run], recv_sem=x_recv.at[run],
                device_id=(to, tile, view), device_id_type=MESH,
            ).start()

        def start(dy, _):
            row = lax.rem(sy + dy, side) * side
            for dx in (2, 1, 3, 0):
                send(row + xs[dx])
            return 0

        lax.fori_loop(1, side, start, 0)
        for dx in (2, 1, 3):
            send(ys[0] + xs[dx])
        for slot in range(lo, hi):
            got[slot, mine, :] = pack[slot, mine, :]

    def await_bytes(ref, sem):
        pltpu.make_async_copy(ref, ref, sem).wait()

    def await_run(run):
        lo, hi = RUNS[run]
        await_bytes(got.at[lo:hi, pl.ds(0, 240)], x_recv.at[run])

    exchange(0)
    tap_copies = []
    for d in (2, 1, 3):
        c = pltpu.make_async_remote_copy(
            src_ref=table, dst_ref=tables.at[view],
            send_sem=tap_send.at[d], recv_sem=tap_recv.at[d],
            device_id=(slab, tile, view_at(d)), device_id_type=MESH,
        )
        c.start()
        tap_copies.append(c)
        pl.semaphore_signal(
            ready, inc=1, device_id=(slab, tile, view_at(d)), device_id_type=MESH
        )
    exchange(1)

    band_z[...] = left3(wide(circulant(taps_z, False)))
    both = wide(circulant(taps_z, True))
    natural[0], natural[1] = both[:, 0:128], both[:, 128:256]
    for zq in range(4):
        rows = [natural[i, pl.ds(zq, 64, stride=4), :] for i in range(2)]
        back_z[64 * zq : 64 * zq + 64, :] = left3(jnp.concatenate(rows, axis=1))
    own_source.wait()
    plane_of = lax.broadcasted_iota(jnp.int32, (256, 256), 0)
    shown = jnp.where(jnp.broadcast_to(source_ref[...], (256, 256)) == plane_of, 1.0, 0.0)
    shown = shown.astype(B16)
    pick[...] = jnp.concatenate([shown, shown], axis=1)
    back_x[...] = right3(circulant(taps_x, False))
    final[...] = jnp.zeros_like(final)
    edges[...] = jnp.zeros_like(edges)

    to_up.wait()
    to_down.wait()
    blur_rows(
        (1, 2),
        jnp.concatenate([band_y[16:32, 0:96], band_y[64:80, 0:96]], axis=0),
        jnp.concatenate([ext[z] for z in range(16)], axis=1),
    )
    exchange(2)
    exchange(3)

    block = lax.broadcasted_iota(jnp.int32, (64, 128), 1) // 32
    half = pl.ds(pl.multiple_of(lax.rem(slab, 2) * 4, 4), 4)

    def process(chunk):
        for run in ((0,), (1, 2), (3,), (4,))[chunk]:
            await_run(run)
        m_high, m_low = split(got[M_SLOT[chunk]])
        routed = dot(pick[...], jnp.concatenate([m_high, m_low], axis=0))
        blurred = dot(band_z[...], right3(got[E_SLOT[chunk]]))
        pulled = dot(back_z[...], right3(routed / blurred))
        by_x = dot(left3(pulled), back_x[...])
        turned = [by_x] + [pltpu.roll(by_x, 32 * m, 1) for m in (1, 2, 3)]
        for w in range(4):
            out = turned[(3 - w) % 4][192:256]
            for zq in (2, 1, 0):
                out = jnp.where(block == zq, turned[(zq - w) % 4][64 * zq : 64 * zq + 64], out)
            forth[chunk, w] = out
        seen[chunk, view, slab // 2, half, :] = forth[
            chunk, view, pl.ds(pl.multiple_of(slab * 4, 4), 4), :
        ]

    def send_quarter(chunk, dv):
        w = view_at(dv)

        def send(to, sem):
            pltpu.make_async_remote_copy(
                src_ref=forth.at[chunk, w, pl.ds(pl.multiple_of(to * 4, 4), 4), :],
                dst_ref=seen.at[chunk, view, slab // 2, half, :],
                send_sem=p_send.at[chunk, sem], recv_sem=p_recv.at[chunk, dv],
                device_id=(to, tile, w), device_id_type=MESH,
            ).start()

        def start(i, _):
            row = lax.rem(sy + lax.rem(4 - i, 3) + 1, side) * side
            for dx in (2, 1, 3, 0):
                send(row + xs[dx], 0)
            return 0

        lax.fori_loop(0, 3, start, 0)
        for dx in (2, 1, 3):
            send(ys[0] + xs[dx], 0)
        if dv:
            send(slab, 1)

    process(0)
    pl.semaphore_wait(ready, 3)
    for dv in (2, 1, 3, 0):
        send_quarter(0, dv)
    exchange(4)
    process(1)
    for dv in (2, 1, 3, 0):
        send_quarter(1, dv)
    process(2)
    for dv in (2, 1, 3, 0):
        send_quarter(2, dv)
    process(3)
    for dv in (2, 1, 3, 0):
        send_quarter(3, dv)

    for c in tap_copies:
        c.wait()
    for v in range(4):
        for t in range(TAPS):
            coefs[v, t] = jnp.broadcast_to(tables[v, pl.ds(t, 1), :], (8, 128))
    for z in range(16):
        quarter[z] = jnp.transpose(ext[z, HALO : 64 + HALO, :])

    first = lax.broadcasted_iota(jnp.int32, (8, 128), 0) < 4

    def accumulate(chunk, dv):
        k = ORDER[chunk]
        v = lax.rem(view + 4 - dv, 4)
        if dv:
            await_bytes(seen.at[chunk, v], p_recv.at[chunk, dv])
        else:
            await_bytes(gauge, p_recv.at[chunk, dv])
        pairs = [seen[chunk, v, j] for j in range(8)]
        swapped = [pltpu.roll(p, 4, 0) for p in pairs]
        odd = [jnp.where(first, swapped[j], swapped[j + 1]) for j in range(7)]
        odd.append(jnp.where(first, swapped[7], 0.0))
        odd.append(jnp.where(first, 0.0, swapped[0]))
        lower = final.at[k - 1] if k else edges.at[0]
        upper = final.at[k + 1] if k < 3 else edges.at[1]
        for ref, kind in ((lower, 1), (upper, -1), (final.at[k], 0)):
            for j in range(8):
                total = None
                for d in range(-RADIUS, RADIUS + 1):
                    i, parity = j + d // 2 - 8 * kind, d % 2
                    if parity:
                        if not -1 <= i <= 7:
                            continue
                        data = odd[i]
                    else:
                        if not 0 <= i <= 7:
                            continue
                        data = pairs[i]
                    term = coefs[v, RADIUS - d] * data
                    total = term if total is None else total + term
                if total is not None:
                    ref[j] = ref[j] + total

    for chunk in range(3):
        for dv in (0, 2, 1, 3):
            accumulate(chunk, dv)
    edge_down = pltpu.make_async_remote_copy(
        src_ref=edges.at[0], dst_ref=arrived.at[0],
        send_sem=edge_send.at[0], recv_sem=edge_recv.at[0],
        device_id=(slab, down, view), device_id_type=MESH,
    )
    edge_up = pltpu.make_async_remote_copy(
        src_ref=edges.at[1], dst_ref=arrived.at[1],
        send_sem=edge_send.at[1], recv_sem=edge_recv.at[1],
        device_id=(slab, up, view), device_id_type=MESH,
    )
    edge_down.start()
    edge_up.start()
    for dv in (0, 2, 1, 3):
        accumulate(3, dv)
    edge_down.wait()
    edge_up.wait()
    final[3] = final[3] + arrived[0]
    final[0] = final[0] + arrived[1]

    own_x = pl.ds(pl.multiple_of(view * 32, 32), 32)
    rows = final.reshape(256, 128)
    for z in range(4):
        turned = jnp.transpose(rows[pl.ds(z, 64, stride=4), :])
        for zq in range(4):
            at = 4 * z + zq
            out_ref[at] = quarter[at, own_x, :] * turned[32 * zq : 32 * zq + 32] * 0.25
    for chunk in range(4):
        await_bytes(got.at[0, pl.ds(0, 240)], p_send.at[chunk, 0])
        await_bytes(gauge.at[pl.ds(0, 3)], p_send.at[chunk, 1])
    for run, (lo, hi) in enumerate(RUNS):
        await_bytes(pack.at[lo:hi, pl.ds(0, 240)], x_send.at[run])


def local(estimate, measured, psf_taps, plane_source, plane_shift):
    dma = pltpu.SemaphoreType.DMA
    vmem = pl.BlockSpec(memory_space=pltpu.VMEM)
    hbm = pl.BlockSpec(memory_space=pl.ANY)
    out = pl.pallas_call(
        kernel,
        name="update",
        out_shape=pltpu.VMEM((16, 32, 64), F32),
        in_specs=[hbm] * 5,
        out_specs=vmem,
        scratch_shapes=[
            pltpu.SMEM((3, 1, TAPS), F32),
            pltpu.SMEM((1, 256), jnp.int32),
            pltpu.VMEM((1, 256), jnp.int32),
            pltpu.VMEM((16, 96, 128), F32),
            pltpu.VMEM((16, 64, 128), F32),
            pltpu.VMEM((8, 256, 128), F32),
            pltpu.VMEM((8, 256, 128), F32),
            pltpu.VMEM((4, 4, 64, 128), F32),
            pltpu.VMEM((4, 4, 8, 8, 128), F32),
            pltpu.VMEM((32, 128), F32),
            pltpu.VMEM((4, 32, 128), F32),
            pltpu.VMEM((4, 32, 8, 128), F32),
            pltpu.VMEM((4, 8, 8, 128), F32),
            pltpu.VMEM((2, 8, 8, 128), F32),
            pltpu.VMEM((2, 8, 8, 128), F32),
            pltpu.VMEM((16, 128, 64), F32),
            pltpu.VMEM((128, 128), F32),
            pltpu.VMEM((384, 128), B16),
            pltpu.VMEM((256, 768), B16),
            pltpu.VMEM((2, 256, 128), F32),
            pltpu.VMEM((256, 768), B16),
            pltpu.VMEM((256, 512), B16),
            pltpu.VMEM((384, 128), B16),
            dma((5,)), dma((2,)), dma((2,)), dma((4,)), dma((4,)),
            dma((5,)), dma((5,)),
            pltpu.VMEM((15, 4, 128), F32),
            dma((4, 2)), dma((4, 4)), dma((2,)), dma((2,)),
            pltpu.SemaphoreType.REGULAR,
        ],
        compiler_params=pltpu.CompilerParams(
            collective_id=0, has_side_effects=True, vmem_limit_bytes=56 * 2**20
        ),
    )(jnp.transpose(psf_taps, (1, 0, 2)), plane_shift, plane_source, estimate, measured)
    return jnp.transpose(out, (0, 2, 1))


def solution(mesh):
    in_specs = (
        P("slab", "tile", None),
        P("view", "slab", "tile", None),
        P("view", None, None),
        P("view", None),
        P("view", None),
    )
    return jax.shard_map(
        local, mesh=mesh, in_specs=in_specs, out_specs=P("slab", "tile", "view"), check_vma=False
    )
```
